32 devices in a mesh: op: 16 (over z, x, core), sec: 2 (over y).
Axes of the slice: x: 2, y: 2, z: 4, core: 2. Of those that a mesh axis runs over, the one named last changes fastest.
Arguments:
- left_ops: float32 [16, 2, 1024, 1024], P('op', 'sec'), may hold values from -0.5 to 3.5
- right_ops: float32 [16, 2, 1024, 1024], P('op', 'sec'), may hold values from -0.5 to 3.5
- amplitudes: float32 [2, 1024, 1024], P('sec', 'op'), may hold values from -72 to 72
- sketch: float32 [1024, 512], replicated, may hold values from -0.1875 to 0.1875
- sector_shift: int32 [16], P('op'), may hold values from 0 to 3
Outputs:
- rotated: float32 [16, 2, 512, 512], P('op', 'sec')
- new_basis: float32 [2, 1024, 512], P('sec', 'op')
- energy: float32 [], replicated
The draws below stay inside these ranges and needn't reach their ends.
Inputs may be any that keep to these rules, and one draw needn't show every extreme that they name: The target sector of pair k from source sector s is (s + sector_shift[k]) mod 2.
All inputs are finite; a program needn't handle non-finite values.
Results may differ from the reference program's by a relative error of at most 0.0003.
Values sent between devices are 32-bit elements; how exact they have to be, the bound alone decides.
A program may use at most 128 MiB of HBM per device.

```python
import jax
import jax.numpy as jnp
from jax import lax

M = 1024
KEEP = 512
PAIRS = 16
SECTORS = 2


def dominant(key):
    key_diag, key_rest = jax.random.split(key)
    jitter = jnp.clip(jax.random.normal(key_rest, (PAIRS, SECTORS, M, M), jnp.float32), -6.0, 6.0)
    diagonal = 10.0 ** jax.random.uniform(key_diag, (PAIRS, SECTORS, M, 1), jnp.float32, -0.3, 0.3)
    identity = jnp.eye(M, dtype=jnp.float32)
    return jitter * (0.5 * M ** (-0.5)) + identity * diagonal


def draw_left_ops(key, part):
    return dominant(jax.random.fold_in(key, 101))


def draw_right_ops(key, part):
    return dominant(jax.random.fold_in(key, 202))


def draw_amplitudes(key, part):
    key_jitter, key_rows, key_cols = jax.random.split(jax.random.fold_in(key, 303), 3)
    jitter = jnp.clip(jax.random.normal(key_jitter, (SECTORS, M, M), jnp.float32), -6.0, 6.0)
    rising = 10.0 ** (jnp.arange(M, dtype=jnp.float32) / M)
    row_rough = jax.random.uniform(key_rows, (SECTORS, M, 1), jnp.float32, 0.5, 1.5)
    col_scale = 10.0 ** jax.random.uniform(key_cols, (SECTORS, 1, M), jnp.float32, 0.0, 0.5)
    return jitter * rising[None, :, None] * row_rough * col_scale / 4.0


def with_ends(result, key, low, largest):
    longest = result.shape.index(max(result.shape))
    spots = []
    for shift in (0, 1):
        where = [jax.random.randint(jax.random.fold_in(key, axis), (), 0, length) for axis, length in enumerate(result.shape)]
        where[longest] = (where[longest] + shift) % result.shape[longest]
        spots.append(tuple(where))
    return result.at[spots[0]].set(low).at[spots[1]].set(largest)


def centred(own_key, extent, scale, limit, kind=jnp.bfloat16):
    entries = jax.random.normal(own_key, extent, jnp.float32) * scale
    return jnp.minimum(jnp.maximum(entries, -limit), limit).astype(kind)


def setup_inputs(seed: int = 0) -> dict:
    arg_keys = jax.random.split(jax.random.key(seed), 6)
    return {
        "left_ops": draw_left_ops(jax.random.fold_in(arg_keys[5], 71), 0),
        "right_ops": draw_right_ops(jax.random.fold_in(arg_keys[5], 71), 0),
        "amplitudes": draw_amplitudes(jax.random.fold_in(arg_keys[5], 71), 0),
        "sketch": centred(arg_keys[3], (M, KEEP), M ** -0.5, 0.1875, jnp.float32),
        "sector_shift": with_ends(jax.random.randint(arg_keys[4], (PAIRS,), 0, 4), jax.random.fold_in(arg_keys[4], 1), 0, 3).astype(jnp.int32),
    }


EXACT = lax.Precision.HIGHEST

def solve_one(factor_one, sketch_one):
    return jax.scipy.linalg.solve_triangular(factor_one, sketch_one.T, lower=True).T

def reference(left_ops, right_ops, amplitudes, sketch, sector_shift):

    def add_pair(running, inputs):
        left_pair, right_pair, offset = inputs

        def per_sector(sector):
            right_part = jnp.dot(amplitudes[sector].astype(jnp.float32), right_pair[sector].astype(jnp.float32), precision=EXACT, preferred_element_type=jnp.float32)
            return jnp.dot(left_pair[sector].astype(jnp.float32), right_part.astype(jnp.float32), precision=EXACT, preferred_element_type=jnp.float32)
        sector_terms = lax.map(per_sector, jnp.arange(SECTORS, dtype=jnp.int32))
        return (running + jnp.roll(sector_terms, offset, axis=0), None)
    product, unused_out = lax.scan(add_pair, jnp.zeros_like(amplitudes), (left_ops, right_ops, sector_shift))
    correlation = jnp.sum(amplitudes * product)
    norm_sq = jnp.sum(amplitudes * amplitudes)
    energy = correlation / norm_sq
    residual = product - energy * amplitudes
    sketched = jnp.einsum('smn,nk->smk', residual, sketch, precision=EXACT)
    gram_mat = jnp.einsum('smk,sml->skl', sketched, sketched, precision=EXACT)
    factor = jnp.linalg.cholesky(gram_mat)
    new_basis = jax.vmap(solve_one)(factor, sketched)

    def rotate(carried, inputs):
        left_pair, offset = inputs
        applied = jnp.einsum('smn,snk->smk', left_pair, new_basis, precision=EXACT)
        target = jnp.roll(new_basis, -offset, axis=0)
        return (carried, jnp.einsum('smk,sml->skl', target, applied, precision=EXACT))
    carried_out, rotated = lax.scan(rotate, jnp.zeros((), jnp.float32), (left_ops, sector_shift))
    return (rotated, new_basis, energy)
```

```python
import functools

import jax
import jax.numpy as jnp
from jax import lax
from jax.experimental import pallas as pl
from jax.experimental.layout import Layout, with_layout_constraint
from jax.experimental.pallas import tpu as pltpu
from jax.sharding import PartitionSpec as P

EXACT = lax.Precision.HIGHEST
SPLIT = lax.Precision.HIGH
HALF = 64
BLOCK = 128


def matmul(first, second, precision=SPLIT):
    return jnp.dot(first, second, precision=precision, preferred_element_type=jnp.float32)


def exact_nn(first, second):
    return lax.dot_general(first, second, (((1,), (0,)), ((), ())), precision=EXACT, preferred_element_type=jnp.float32)


def exact_nt(first, second):
    return lax.dot_general(first, second, (((1,), (1,)), ((), ())), precision=EXACT, preferred_element_type=jnp.float32)


def eliminate_many(blocks):
    sub = lax.broadcasted_iota(jnp.int32, (8, BLOCK), 0)
    lane = lax.broadcasted_iota(jnp.int32, (8, BLOCK), 1)
    rows = [[block[8 * c : 8 * c + 8, :] for c in range(HALF // 8)] for block in blocks]
    for j in range(0, HALF, 2):
        home = j // 8
        for chunk in rows:
            row = chunk[home][j % 8 : j % 8 + 1, :]
            follower = chunk[home][j % 8 + 1 : j % 8 + 2, :]
            head = jnp.broadcast_to(row[:, j : j + 1], (1, BLOCK))
            cross = jnp.broadcast_to(row[:, j + 1 : j + 2], (1, BLOCK))
            tail = jnp.broadcast_to(follower[:, j + 1 : j + 2], (1, BLOCK))
            head_inverse = 1.0 / head
            ratio = cross * head_inverse
            scaled = row * head_inverse
            reduced = follower - cross * scaled
            reduced_scaled = reduced * (head / (head * tail - cross * cross))
            for c in range(home, HALF // 8):
                column = jnp.broadcast_to(chunk[c][:, j : j + 1], (8, BLOCK))
                beside = jnp.broadcast_to(chunk[c][:, j + 1 : j + 2], (8, BLOCK)) - column * ratio
                if c == home:
                    column = jnp.where(sub > j % 8, column, 0.0)
                    beside = jnp.where(sub > j % 8 + 1, beside, 0.0)
                chunk[c] = chunk[c] - column * scaled - beside * reduced_scaled
    results = []
    for chunk in rows:
        scaled_chunks = []
        for c in range(HALF // 8):
            pivot = jnp.sum(jnp.where(lane == sub + 8 * c, chunk[c], 0.0), axis=1, keepdims=True)
            scaled_chunks.append(jnp.where(lane >= HALF, chunk[c] * lax.rsqrt(pivot), 0.0))
        results.append(jnp.concatenate(scaled_chunks, axis=0))
    return results


def invert_blocks(blocks):
    lane = lax.broadcasted_iota(jnp.int32, (HALF, BLOCK), 1)
    row = lax.broadcasted_iota(jnp.int32, (HALF, BLOCK), 0)
    unit = jnp.where(lane == row + HALF, 1.0, 0.0)
    empty = jnp.zeros((HALF, BLOCK), jnp.float32)

    def tall(top):
        return jnp.concatenate([top, empty], axis=0)

    first = eliminate_many([jnp.where(lane < HALF, block[:HALF], unit) for block in blocks])
    upper = [pltpu.roll(one, HALF, 1) for one in first]
    lower = [block[HALF:] for block in blocks]
    coupling = [exact_nt(low, tall(up)) for low, up in zip(lower, upper)]
    schur = [pltpu.roll(low, HALF, 1) - exact_nt(mid, tall(mid)) for low, mid in zip(lower, coupling)]
    second = eliminate_many([jnp.where(lane < HALF, one, unit) for one in schur])
    result = []
    for up, mid, right in zip(upper, coupling, second):
        carried = exact_nn(mid, tall(up))
        left = exact_nn(pltpu.roll(right, HALF, 1), tall(carried))
        result.append(jnp.concatenate([up, right - left], axis=0))
    return result


def inverse_factor_kernel(count, order, gram_ref, inverse_ref, work):
    row = lax.broadcasted_iota(jnp.int32, (order, order), 0)
    column = lax.broadcasted_iota(jnp.int32, (order, order), 1)
    for i in range(count):
        work[i] = gram_ref[i]
        inverse_ref[i] = jnp.where(row == column, 1.0, 0.0)
    tall_row = lax.broadcasted_iota(jnp.int32, (order, BLOCK), 0)

    def step(b, carry):
        start = pl.multiple_of(b * BLOCK, BLOCK)
        here = pl.ds(start, BLOCK)
        inverses = invert_blocks([work[i, here, here] for i in range(count)])
        for i in range(count):
            panel = jnp.where(tall_row >= start + BLOCK, work[i, :, here], 0.0)
            low = exact_nt(panel, inverses[i])
            strip = exact_nn(inverses[i], inverse_ref[i, here, :])
            inverse_ref[i] = inverse_ref[i] - exact_nn(low, strip)
            inverse_ref[i, here, :] = strip
            work[i] = work[i] - exact_nt(low, low)
        return carry

    lax.fori_loop(0, order // BLOCK, step, 0)


def inverse_factors(gram_pair):
    count, order, _ = gram_pair.shape
    return pl.pallas_call(
        functools.partial(inverse_factor_kernel, count, order),
        out_shape=jax.ShapeDtypeStruct(gram_pair.shape, jnp.float32),
        in_specs=[pl.BlockSpec(memory_space=pltpu.VMEM)],
        out_specs=pl.BlockSpec(memory_space=pltpu.VMEM),
        scratch_shapes=[pltpu.VMEM(gram_pair.shape, jnp.float32)],
        cost_estimate=pl.CostEstimate(flops=40 * order**3, bytes_accessed=8 * order**2, transcendentals=0),
        name="inverse_factors",
    )(gram_pair)


def split(value):
    high = value.astype(jnp.bfloat16)
    return high, (value - high.astype(jnp.float32)).astype(jnp.bfloat16)


def product(high, low, other_high, other_low):
    def one(first, second):
        return lax.dot_general(first, second, (((1,), (0,)), ((), ())), preferred_element_type=jnp.float32)

    return one(high, other_high) + (one(high, other_low) + one(low, other_high))


def ring_chip(position, chips):
    return 2 * position + lax.div(position, chips // 2) * (2 * chips - 1 - 4 * position)


def front_kernel(
    sizes, left_ref, right_ref, slab_ref, sketch_ref, choice_ref,
    sketched_ref, energy_ref,
    held, other, left_full, right_full, sketch_full, left_high, left_low, weight_high, weight_low,
    part_high, part_low, image_high, image_low, second, term, term_out, term_in, outgoing, incoming,
    full_in, mail_out, mail_in, tile_out, tile_in, sums, choice_there,
    local_sem, choice_sem, ring_send, ring_recv, pair_send, pair_recv, cross_send, cross_recv, term_send, term_recv,
    sum_send, sum_recv, full_send, full_recv, mail_send, mail_recv, tile_send, tile_recv,
    again_send, again_recv, both_send, both_recv,
):
    chips, sectors, reach, height, order, keep, pieces = sizes
    op = lax.axis_index("op")
    sec = lax.axis_index("sec")
    core = lax.rem(op, 2)
    chip = lax.div(op, 2)
    lower = lax.div(chip, 2)
    position = lower + lax.rem(chip, 2) * (chips - 1 - 2 * lower)
    way = 1 - 2 * core

    def chip_at(steps, turn):
        return ring_chip(lax.rem(position + chips + turn * steps, chips), chips)

    ahead = {"op": 2 * chip_at(1, way) + core, "sec": sec}
    behind = {"op": 2 * chip_at(1, -way) + core, "sec": sec}
    sibling = {"op": 2 * chip + 1 - core, "sec": sec}

    def sector(distance):
        return {"op": op, "sec": lax.rem(sec + distance, sectors)}

    def remote(source, target, send, recv, device):
        return pltpu.make_async_remote_copy(
            src_ref=source, dst_ref=target, send_sem=send, recv_sem=recv, device_id=device, device_id_type=pl.DeviceIdType.MESH
        )

    started = []

    def start(copy):
        copy.start()
        started.append(copy)

    pairs = [(m, chips - m) for m in range(1, chips // 2)] + [(chips // 2, 0)]
    blocks = [m for pair in pairs for m in pair]
    copies = [
        pltpu.make_async_copy(slab_ref, held.at[0, 0], local_sem.at[0]),
        pltpu.make_async_copy(sketch_ref, sketch_full, local_sem.at[1]),
        pltpu.make_async_copy(right_ref, right_full, local_sem.at[2]),
    ]
    for copy in copies:
        copy.start()
    for place, m in enumerate(blocks):
        base = chip_at(m, -way) * 2 * height
        for side in (0, 1):
            begin = pl.multiple_of(base + (core if side == 0 else 1 - core) * height, height)
            pltpu.make_async_copy(
                left_ref.at[pl.ds(begin, height)], left_full.at[pl.ds((2 * place + side) * height, height)], local_sem.at[3]
            ).start()

    barrier = pltpu.get_barrier_semaphore()
    greeted = [ahead, behind, sibling] + [sector(d) for d in range(1, sectors)]
    for device in greeted:
        pl.semaphore_signal(barrier, inc=1, device_id=device, device_id_type=pl.DeviceIdType.MESH)
    pl.semaphore_wait(barrier, len(greeted))

    part = height // pieces

    def ring_copy(j, p):
        rows = pl.ds(p * part, part)
        return remote(held.at[0, j, rows], held.at[0, j + 1, rows], ring_send.at[j, p], ring_recv.at[j, p], ahead)

    def pair_copy(j, p):
        rows = pl.ds(p * part, part)
        return remote(held.at[0, j, rows], held.at[1, j, rows], pair_send.at[j, p], pair_recv.at[j, p], sibling)

    def cross_copy(d, j):
        return remote(
            held.at[0, j], other.at[d - 1, j], cross_send.at[d - 1, j], cross_recv.at[d - 1, j], sector(sectors - d)
        )

    def cross_start(j):
        for d in range(1, reach):
            start(cross_copy(d, j))

    copies[0].wait()
    for p in range(pieces):
        start(ring_copy(0, p))
        start(pair_copy(0, p))
    choice_copy = remote(choice_ref, choice_there, choice_sem.at[0], choice_sem.at[1], sibling)
    start(choice_copy)
    cross_start(0)

    batch = 4 * height
    tile = min(512, keep)
    urgent, later = [], []

    def run(budget):
        while budget > 0 and (urgent or later):
            cost, work = (urgent or later).pop(0)
            work()
            budget -= cost

    def split_rows(source, high, low, first, count, columns):
        step = 32

        def one(i, carry):
            rows = pl.ds(pl.multiple_of(first + i * step, step), step)
            high[rows, columns], low[rows, columns] = split(source[rows, :])
            return carry

        lax.fori_loop(0, count // step, one, 0)

    def sketch_work():
        copies[1].wait()
        split_rows(sketch_full, weight_high, weight_low, 0, order, pl.ds(order + keep, keep))

    def right_work(i):
        if i == 0:
            copies[2].wait()
        split_rows(right_full, weight_high, weight_low, i * batch, batch, pl.ds(0, order))
        rows = pl.ds(i * batch, batch)
        inner = pl.ds(0, order)
        last = pl.ds(order + keep, keep)
        high, low = split(product(weight_high[rows, inner], weight_low[rows, inner], weight_high[:, last], weight_low[:, last]))
        weight_high[rows, pl.ds(order, keep)] = high
        weight_low[rows, pl.ds(order, keep)] = low

    def left_work(i):
        if i == 0:
            pltpu.make_async_copy(left_ref, left_full, local_sem.at[3]).wait()
        split_rows(left_full, left_high, left_low, i * batch, batch, pl.ds(0, order))

    def slabs_of(b):
        for level in (2 * b, 2 * b + 1):
            yield 0, level, chip_at(level, -way) * 2 + core
            yield 1, level, chip_at(level, way) * 2 + 1 - core

    def image_columns(b, columns):
        result = product(part_high[b], part_low[b], weight_high[:, columns], weight_low[:, columns])
        high, low = split(result)
        for i, (_, _, slab) in enumerate(slabs_of(b)):
            rows = pl.ds(pl.multiple_of(slab * height, height), height)
            image_high[rows, columns] = high[i * height : (i + 1) * height]
            image_low[rows, columns] = low[i * height : (i + 1) * height]

    def split_work(b):
        for i, (side, level, _) in enumerate(slabs_of(b)):
            if side == 1:
                for p in range(pieces):
                    pair_copy(level, p).wait_recv()
            high, low = split(held[side, level])
            part_high[b, pl.ds(i * height, height)] = high
            part_low[b, pl.ds(i * height, height)] = low
        for column in range(0, keep, tile):
            image_columns(b, pl.ds(order + column, tile))

    def image_work(b, column):
        image_columns(b, pl.ds(column, tile))

    def second_work(b, column):
        weights = pl.ds(order + keep + column, tile)
        second[b, :, pl.ds(column, tile)] = product(part_high[b], part_low[b], weight_high[:, weights], weight_low[:, weights])

    unit = 0.75
    urgent.append((0.9, sketch_work))
    for i in range(order // batch):
        urgent.append((1.2, functools.partial(right_work, i)))
    for i in range(order // batch):
        urgent.append((0.5, functools.partial(left_work, i)))

    crossing = 1
    for j in range(1, chips):
        for p in range(pieces):
            ring_copy(j - 1, p).wait_recv()
            if j < chips - 1:
                start(ring_copy(j, p))
            start(pair_copy(j, p))
            if p == pieces - 1 and j % 2 == 0:
                cross_start(crossing)
                crossing += 1
            if p == pieces - 1 and j % 2 == 1:
                b = j // 2
                urgent.append((unit + 0.5, functools.partial(split_work, b)))
                for column in range(0, order, tile):
                    later.append((unit, functools.partial(image_work, b, column)))
                for column in range(0, keep, tile):
                    later.append((unit, functools.partial(second_work, b, column)))
            if j < chips - 1 or p < pieces - 1:
                run(2.8 / pieces)
    while urgent:
        urgent.pop(0)[1]()

    choice_copy.wait_recv()

    def chosen(d, mine, there, shape):
        own = jnp.broadcast_to(choice_ref[0:1, 0:1], shape) == float(d)
        far = jnp.broadcast_to(choice_there[0:1, 0:1], shape) == float(d)
        return jnp.where(own, mine, 0.0) + jnp.where(far, there, 0.0)

    def term_copy(m):
        return remote(term_out.at[m], term_in.at[m], term_send.at[m], term_recv.at[m], sibling)

    def full_copy(m):
        return remote(left_full.at[pl.ds((chips + m) * height, height)], full_in.at[m], full_send.at[m], full_recv.at[m], sibling)

    def halves(i, result):
        for k, m in enumerate(pairs[i]):
            own = result[2 * k * height : (2 * k + 1) * height]
            yield m, own, (chips - m) % chips, result[(2 * k + 1) * height : (2 * k + 2) * height]

    def rows_of(i):
        return pl.ds(i * batch, batch)

    def term_work(i):
        for column in range(0, keep, tile):
            inner = pl.ds(order + column, tile)
            result = product(left_high[rows_of(i)], left_low[rows_of(i)], image_high[:, inner], image_low[:, inner])
            for m, own, there, far in halves(i, result):
                term[m, :, pl.ds(column, tile)] = own
                term_out[there, :, pl.ds(column, tile)] = far
        for m in pairs[i]:
            start(term_copy((chips - m) % chips))

    def full_work(i, column):
        inner = pl.ds(column, tile)
        result = product(left_high[rows_of(i)], left_low[rows_of(i)], image_high[:, inner], image_low[:, inner])
        for m, own, there, far in halves(i, result):
            left_full[pl.ds(m * height, height), inner] = own
            left_full[pl.ds((chips + there) * height, height), inner] = far
        if column + tile == order:
            for m in pairs[i]:
                start(full_copy((chips - m) % chips))

    done_terms = []
    for i in range(len(pairs)):
        urgent.append((unit + 0.1, lambda i=i: (term_work(i), done_terms.append(i))))
    for i in range(len(pairs)):
        for column in range(0, order, tile):
            later.append((unit, functools.partial(full_work, i, column)))

    def sum_copy(r, d):
        return remote(outgoing.at[r, d], incoming.at[r, d], sum_send.at[r, d], sum_recv.at[r, d], ahead)

    shape = (height, keep)
    for r in range(chips - 1):
        m = r + 1
        while min(m, chips - m) - 1 not in done_terms:
            urgent.pop(0)[1]()
        term_copy(m).wait_recv()
        for d in range(reach):
            value = chosen(d, term[m], term_in[m], shape)
            if r > 0:
                sum_copy(r - 1, d).wait_recv()
                value = value + incoming[r - 1, d]
            outgoing[r, d] = value
            start(sum_copy(r, d))
            if d == reach - 1 and r % 2 == 0 and crossing < chips:
                cross_start(crossing)
                crossing += 1
            run(2.8 / reach)
    while crossing < chips:
        cross_start(crossing)
        crossing += 1
    while urgent or later:
        (urgent or later).pop(0)[1]()

    def mail_copy(d):
        return remote(mail_out.at[d - 1], mail_in.at[d - 1], mail_send.at[d - 1], mail_recv.at[d - 1], sector(d))

    def tile_copy(d):
        return remote(tile_out, tile_in.at[d - 1], tile_send.at[d - 1], tile_recv.at[d - 1], sector(d))

    term_copy(0).wait_recv()
    for d in reversed(range(reach)):
        sum_copy(chips - 2, d).wait_recv()
        value = chosen(d, term[0], term_in[0], shape) + incoming[chips - 2, d]
        if d > 0:
            mail_out[d - 1] = value
            start(mail_copy(d))
        else:
            sums[0, 0, pl.ds(0, height)] = value

    small = (8, order)
    total = jnp.zeros(small, jnp.float32)
    for m in range(chips):
        full_copy(m).wait_recv()
        for d in range(1, reach):
            cross_copy(d, m).wait_recv()

        def add(i, carry, m=m):
            rows = pl.ds(pl.multiple_of(i * 8, 8), 8)
            for d in range(reach):
                state = held[0, m, rows] if d == 0 else other[d - 1, m, rows]
                carry = carry + state * chosen(d, left_full[pl.ds(pl.multiple_of(m * height + i * 8, 8), 8)], full_in[m, rows], small)
            return carry

        total = lax.fori_loop(0, height // 8, add, total)
    own = held[0, 0]
    up = jnp.broadcast_to(jnp.sum(total, keepdims=True), (8, keep))
    down = jnp.broadcast_to(jnp.sum(own * own, keepdims=True), (8, keep))
    row = lax.broadcasted_iota(jnp.int32, (8, keep), 0)
    tile_out[...] = jnp.where(row == 0, up, down)
    for d in range(1, sectors):
        start(tile_copy(d))
    for d in range(1, reach):
        mail_copy(d).wait_recv()
        sums[0, 0, pl.ds(0, height)] += mail_in[d - 1]
    both = tile_out[...]
    for d in range(1, sectors):
        tile_copy(d).wait_recv()
        both = both + tile_in[d - 1]
    sums[0, 0, pl.ds(height, 8)] = both

    spans = [pl.ds(p * part, part if p < pieces - 1 else part + 8) for p in range(pieces)]

    def again_copy(j, p):
        return remote(sums.at[0, j, spans[p]], sums.at[0, j + 1, spans[p]], again_send.at[j, p], again_recv.at[j, p], ahead)

    def both_copy(j, p):
        return remote(sums.at[0, j, spans[p]], sums.at[1, j, spans[p]], both_send.at[j, p], both_recv.at[j, p], sibling)

    for j in range(chips):
        for p in range(pieces):
            if j > 0:
                again_copy(j - 1, p).wait_recv()
            if j < chips - 1:
                start(again_copy(j, p))
            start(both_copy(j, p))
    for j in range(chips):
        for p in range(pieces):
            both_copy(j, p).wait_recv()

    both = jnp.zeros((8, keep), jnp.float32)
    for j in range(chips):
        for side in (0, 1):
            both = both + sums[side, j, pl.ds(height, 8)]
    energy = both[0:1] / both[1:2]
    energy_ref[...] = jnp.broadcast_to(energy, (8, keep))
    for b in range(chips // 2):
        for i, (side, level, slab) in enumerate(slabs_of(b)):
            rows = pl.ds(pl.multiple_of(slab * height, height), height)
            minus = energy * second[b, pl.ds(i * height, height)]
            sketched_ref[rows, :] = sums[side, level, pl.ds(0, height)] - minus
    for copy in started:
        copy.wait_send()


def front(left_op, right_op, slab, sketch, choice):
    height, order = slab.shape
    keep = sketch.shape[1]
    sectors = lax.axis_size("sec")
    chips = lax.axis_size("op") // 2
    reach = min(4, sectors)
    pieces = 2
    wide, half = jnp.float32, jnp.bfloat16
    columns = order + keep
    batch = 4 * height
    dma = pltpu.SemaphoreType.DMA
    scratch = [
        ((2, chips, height, order), wide), ((reach - 1, chips, height, order), wide), ((order, order), wide),
        ((order, order), wide), ((order, keep), wide), ((order, order), half), ((order, order), half),
        ((order, columns + keep), half), ((order, columns + keep), half),
        ((chips // 2, batch, order), half), ((chips // 2, batch, order), half), ((order, columns), half), ((order, columns), half),
        ((chips // 2, batch, keep), wide), ((chips, height, keep), wide), ((chips, height, keep), wide),
        ((chips, height, keep), wide), ((chips - 1, reach, height, keep), wide), ((chips - 1, reach, height, keep), wide),
        ((chips, height, order), wide),
        ((reach - 1, height, keep), wide), ((reach - 1, height, keep), wide), ((8, keep), wide), ((sectors - 1, 8, keep), wide),
        ((2, chips, height + 8, keep), wide), ((8, 128), wide),
    ]
    counts = [
        (4,), (2,), (chips - 1, pieces), (chips - 1, pieces), (chips, pieces), (chips, pieces), (reach - 1, chips),
        (reach - 1, chips), (chips,), (chips,), (chips - 1, reach), (chips - 1, reach), (chips,), (chips,), (reach - 1,),
        (reach - 1,), (sectors - 1,), (sectors - 1,), (chips - 1, pieces), (chips - 1, pieces), (chips, pieces), (chips, pieces),
    ]
    anywhere = pl.BlockSpec(memory_space=pl.ANY)
    inside = pl.BlockSpec(memory_space=pltpu.VMEM)
    sizes = (chips, sectors, reach, height, order, keep, pieces)
    return pl.pallas_call(
        functools.partial(front_kernel, sizes),
        out_shape=(jax.ShapeDtypeStruct((order, keep), wide), jax.ShapeDtypeStruct((8, keep), wide)),
        in_specs=[anywhere] * 4 + [inside],
        out_specs=(inside, inside),
        scratch_shapes=[pltpu.VMEM(shape, kind) for shape, kind in scratch] + [dma(count) for count in counts],
        compiler_params=pltpu.CompilerParams(collective_id=0, has_side_effects=True, vmem_limit_bytes=60 * 2**20),
        cost_estimate=pl.CostEstimate(flops=24 * order**3, bytes_accessed=48 * order**2, transcendentals=0),
        name="front",
    )(left_op, right_op, slab, sketch, choice)


def shifted(block, axis, distance):
    devices = range(lax.axis_size(axis))
    route = [((i - distance) % len(devices), i) for i in devices]
    return lax.ppermute(block, axis, route)


def from_target(block, choice, reach):
    result = block
    for distance in range(1, reach):
        result = jnp.where(choice == distance, shifted(block, "sec", -distance), result)
    return result


def row_major(block):
    return with_layout_constraint(block, Layout(major_to_minor=tuple(range(block.ndim))))


def from_target_halves(block, choice, reach, beside=()):
    slabs = lax.axis_size("op")
    half = block.shape[0] // 2
    side = lax.rem(lax.axis_index("op"), 2)
    share = row_major(lax.dynamic_slice_in_dim(block, side * half, half, 0))
    result = block
    for distance in range(1, reach):
        mine = shifted(share, "sec", -distance)
        if beside:
            mine, *beside = lax.optimization_barrier((mine, *beside))
        other = lax.ppermute(mine, "op", [(i, i ^ 1) for i in range(slabs)])
        whole = jnp.concatenate([jnp.where(side == 0, mine, other), jnp.where(side == 0, other, mine)], axis=0)
        result = jnp.where(choice == distance, whole, result)
    return result, beside


def body(left_ops, right_ops, amplitudes, sketch, sector_shift):
    left_op = left_ops[0, 0]
    sectors = lax.axis_size("sec")
    height = amplitudes.shape[1]
    choice = lax.rem(sector_shift[0], sectors)
    reach = min(4, sectors)
    flag = jnp.full((8, 128), choice.astype(jnp.float32))
    sketched, quotient = front(left_op, right_ops[0, 0], amplitudes[0], sketch, flag)
    energy = quotient[0, 0]
    sketched_there = from_target(sketched, choice, reach)
    gram_mat = jnp.einsum("rk,rl->kl", sketched, sketched, precision=EXACT)
    inverse = inverse_factors(gram_mat[None])[0]
    basis = lax.dot_general(sketched, inverse, (((1,), (1,)), ((), ())), precision=SPLIT)
    basis_slab = lax.dynamic_slice_in_dim(basis, lax.axis_index("op") * height, height, 0)
    applied = matmul(left_op, basis)
    inverse_there, (applied,) = from_target_halves(inverse, choice, reach, (applied,))
    unscaled = jnp.einsum("rk,rl->kl", sketched_there, applied, precision=SPLIT)
    rotated = matmul(inverse_there, unscaled)
    return (rotated[None, None], basis_slab[None], energy)


def solution(mesh):
    in_specs = (
        P("op", "sec", None, None),
        P("op", "sec", None, None),
        P("sec", "op", None),
        P(),
        P("op"),
    )
    out_specs = (P("op", "sec", None, None), P("sec", "op", None), P())
    return jax.shard_map(body, mesh=mesh, in_specs=in_specs, out_specs=out_specs, check_vma=False)
```

```python
import functools

import jax
import jax.numpy as jnp
from jax import lax
from jax.experimental import pallas as pl
from jax.experimental.pallas import tpu as pltpu
from jax.sharding import PartitionSpec as P

EXACT = lax.Precision.HIGHEST
HALF = 64
BLOCK = 128


def exact_nn(first, second):
    return lax.dot_general(first, second, (((1,), (0,)), ((), ())), precision=EXACT, preferred_element_type=jnp.float32)


def exact_nt(first, second):
    return lax.dot_general(first, second, (((1,), (1,)), ((), ())), precision=EXACT, preferred_element_type=jnp.float32)


def eliminate_many(blocks):
    sub = lax.broadcasted_iota(jnp.int32, (8, BLOCK), 0)
    lane = lax.broadcasted_iota(jnp.int32, (8, BLOCK), 1)
    rows = [[block[8 * c : 8 * c + 8, :] for c in range(HALF // 8)] for block in blocks]
    for j in range(0, HALF, 2):
        home = j // 8
        for chunk in rows:
            row = chunk[home][j % 8 : j % 8 + 1, :]
            follower = chunk[home][j % 8 + 1 : j % 8 + 2, :]
            head = jnp.broadcast_to(row[:, j : j + 1], (1, BLOCK))
            cross = jnp.broadcast_to(row[:, j + 1 : j + 2], (1, BLOCK))
            tail = jnp.broadcast_to(follower[:, j + 1 : j + 2], (1, BLOCK))
            head_inverse = 1.0 / head
            ratio = cross * head_inverse
            scaled = row * head_inverse
            reduced = follower - cross * scaled
            reduced_scaled = reduced * (head / (head * tail - cross * cross))
            for c in range(home, HALF // 8):
                column = jnp.broadcast_to(chunk[c][:, j : j + 1], (8, BLOCK))
                beside = jnp.broadcast_to(chunk[c][:, j + 1 : j + 2], (8, BLOCK)) - column * ratio
                if c == home:
                    column = jnp.where(sub > j % 8, column, 0.0)
                    beside = jnp.where(sub > j % 8 + 1, beside, 0.0)
                chunk[c] = chunk[c] - column * scaled - beside * reduced_scaled
    results = []
    for chunk in rows:
        scaled_chunks = []
        for c in range(HALF // 8):
            pivot = jnp.sum(jnp.where(lane == sub + 8 * c, chunk[c], 0.0), axis=1, keepdims=True)
            scaled_chunks.append(jnp.where(lane >= HALF, chunk[c] * lax.rsqrt(pivot), 0.0))
        results.append(jnp.concatenate(scaled_chunks, axis=0))
    return results


def invert_blocks(blocks):
    lane = lax.broadcasted_iota(jnp.int32, (HALF, BLOCK), 1)
    row = lax.broadcasted_iota(jnp.int32, (HALF, BLOCK), 0)
    unit = jnp.where(lane == row + HALF, 1.0, 0.0)
    empty = jnp.zeros((HALF, BLOCK), jnp.float32)

    def tall(top):
        return jnp.concatenate([top, empty], axis=0)

    first = eliminate_many([jnp.where(lane < HALF, block[:HALF], unit) for block in blocks])
    upper = [pltpu.roll(one, HALF, 1) for one in first]
    lower = [block[HALF:] for block in blocks]
    coupling = [exact_nt(low, tall(up)) for low, up in zip(lower, upper)]
    schur = [pltpu.roll(low, HALF, 1) - exact_nt(mid, tall(mid)) for low, mid in zip(lower, coupling)]
    second = eliminate_many([jnp.where(lane < HALF, one, unit) for one in schur])
    result = []
    for up, mid, right in zip(upper, coupling, second):
        carried = exact_nn(mid, tall(up))
        left = exact_nn(pltpu.roll(right, HALF, 1), tall(carried))
        result.append(jnp.concatenate([up, right - left], axis=0))
    return result


def split(value):
    high = value.astype(jnp.bfloat16)
    return high, (value - high.astype(jnp.float32)).astype(jnp.bfloat16)


def product(high, low, other_high, other_low, contract=((1,), (0,))):
    def one(first, second):
        return lax.dot_general(first, second, (contract, ((), ())), preferred_element_type=jnp.float32)

    return one(high, other_high) + (one(high, other_low) + one(low, other_high))


def ring_chip(position, chips):
    return 2 * position + lax.div(position, chips // 2) * (2 * chips - 1 - 4 * position)


def front_kernel(
    sizes, left_ref, right_ref, slab_ref, sketch_ref, choice_ref,
    rotated_ref, basis_ref, energy_ref,
    held, other, left_full, right_full, sketch_full, left_high, left_low, weight_high, weight_low,
    part_high, part_low, image_high, image_low, second, term, term_out, term_in, outgoing, incoming,
    mail_out, mail_in, tile_out, tile_in, sums, choice_there, pivot_out, mid_high, mid_low,
    local_sem, choice_sem, ring_send, ring_recv, pair_send, pair_recv, cross_send, cross_recv, term_send, term_recv,
    sum_send, sum_recv, full_send, full_recv, mail_send, mail_recv, tile_send, tile_recv,
    again_send, again_recv, both_send, both_recv, far_send, far_recv, near_send, near_recv, strip_send, strip_recv, pivot_send,
    pivot_recv,
):
    chips, sectors, reach, height, order, keep, pieces = sizes
    op = lax.axis_index("op")
    sec = lax.axis_index("sec")
    core = lax.rem(op, 2)
    chip = lax.div(op, 2)
    lower = lax.div(chip, 2)
    position = lower + lax.rem(chip, 2) * (chips - 1 - 2 * lower)
    way = 1 - 2 * core

    def chip_at(steps, turn):
        return ring_chip(lax.rem(position + chips + turn * steps, chips), chips)

    ahead = {"op": 2 * chip_at(1, way) + core, "sec": sec}
    behind = {"op": 2 * chip_at(1, -way) + core, "sec": sec}
    sibling = {"op": 2 * chip + 1 - core, "sec": sec}

    def sector(distance):
        return {"op": op, "sec": lax.rem(sec + distance, sectors)}

    def remote(source, target, send, recv, device):
        return pltpu.make_async_remote_copy(
            src_ref=source, dst_ref=target, send_sem=send, recv_sem=recv, device_id=device, device_id_type=pl.DeviceIdType.MESH
        )

    started = []

    def start(copy):
        copy.start()
        started.append(copy)

    pairs = [(m, chips - m) for m in range(1, chips // 2)] + [(chips // 2, 0)]
    orders = pairs[::-1]
    blocks = [m for pair in orders for m in pair]
    copies = [
        pltpu.make_async_copy(slab_ref, held.at[0, 0], local_sem.at[0]),
        pltpu.make_async_copy(sketch_ref, sketch_full, local_sem.at[1]),
        pltpu.make_async_copy(right_ref, right_full, local_sem.at[2]),
    ]
    for copy in copies:
        copy.start()
    for place, m in enumerate(blocks):
        base = chip_at(m, -way) * 2 * height
        for side in (0, 1):
            begin = pl.multiple_of(base + (core if side == 0 else 1 - core) * height, height)
            pltpu.make_async_copy(
                left_ref.at[pl.ds(begin, height)], left_full.at[pl.ds((2 * place + side) * height, height)], local_sem.at[3]
            ).start()

    barrier = pltpu.get_barrier_semaphore()
    greeted = [ahead, behind, sibling] + [sector(d) for d in range(1, sectors)]
    for device in greeted:
        pl.semaphore_signal(barrier, inc=1, device_id=device, device_id_type=pl.DeviceIdType.MESH)
    pl.semaphore_wait(barrier, len(greeted))

    part = height // pieces

    def onward(buffer, m, rows, send, recv):
        source, device = (m - 1, ahead) if m <= chips // 2 else ((m + 1) % chips, behind)
        return remote(buffer.at[0, source, rows], buffer.at[0, m, rows], send, recv, device)

    def after(m):
        if m == 0:
            return [1, chips - 1]
        if m < chips // 2:
            return [m + 1]
        return [m - 1] if m > chips // 2 + 1 else []

    def ring_copy(m, p):
        return onward(held, m, pl.ds(p * part, part), ring_send.at[m - 1, p], ring_recv.at[m - 1, p])

    def pair_copy(m, p):
        rows = pl.ds(p * part, part)
        return remote(held.at[0, m, rows], held.at[1, m, rows], pair_send.at[m, p], pair_recv.at[m, p], sibling)

    def cross_copy(d, j):
        return remote(
            held.at[0, j], other.at[d - 1, pl.ds(j * height, height)], cross_send.at[d - 1, j], cross_recv.at[d - 1, j], sector(sectors - d)
        )

    crossing = [0] + [m for pair in pairs[:-1] for m in pair] + [chips // 2]

    def cross_start():
        if crossing:
            m = crossing.pop(0)
            for d in range(1, reach):
                start(cross_copy(d, m))

    copies[0].wait()
    for p in range(pieces):
        for m in after(0):
            start(ring_copy(m, p))
        start(pair_copy(0, p))
    choice_copy = remote(choice_ref, choice_there, choice_sem.at[0], choice_sem.at[1], sibling)
    start(choice_copy)
    cross_start()

    batch = 4 * height
    tile = min(512, keep)
    urgent, later = [], []

    def run(budget):
        while budget > 0 and (urgent or later):
            cost, work = (urgent or later).pop(0)
            work()
            budget -= cost

    def split_rows(source, high, low, first, count, columns):
        step = 32

        def one(i, carry):
            rows = pl.ds(pl.multiple_of(first + i * step, step), step)
            high[rows, columns], low[rows, columns] = split(source[rows, :])
            return carry

        lax.fori_loop(0, count // step, one, 0)

    def sketch_work():
        copies[1].wait()
        split_rows(sketch_full, weight_high, weight_low, 0, order, pl.ds(order + keep, keep))

    def right_work(i):
        if i == 0:
            copies[2].wait()
        split_rows(right_full, weight_high, weight_low, i * batch, batch, pl.ds(0, order))
        rows = pl.ds(i * batch, batch)
        inner = pl.ds(0, order)
        last = pl.ds(order + keep, keep)
        high, low = split(product(weight_high[rows, inner], weight_low[rows, inner], weight_high[:, last], weight_low[:, last]))
        weight_high[rows, pl.ds(order, keep)] = high
        weight_low[rows, pl.ds(order, keep)] = low

    def left_work(i):
        if i == 0:
            pltpu.make_async_copy(left_ref, left_full, local_sem.at[3]).wait()
        split_rows(left_full, left_high, left_low, i * batch, batch, pl.ds(0, order))

    def slabs_of(b):
        for m in pairs[b]:
            yield 0, m, chip_at(m, -way) * 2 + core
            yield 1, m, chip_at(m, way) * 2 + 1 - core

    def image_columns(b, columns):
        result = product(part_high[b], part_low[b], weight_high[:, columns], weight_low[:, columns])
        high, low = split(result)
        for i, (_, _, slab) in enumerate(slabs_of(b)):
            rows = pl.ds(pl.multiple_of(slab * height, height), height)
            image_high[rows, columns] = high[i * height : (i + 1) * height]
            image_low[rows, columns] = low[i * height : (i + 1) * height]

    def split_work(b):
        for i, (side, level, _) in enumerate(slabs_of(b)):
            if side == 1:
                for p in range(pieces):
                    pair_copy(level, p).wait_recv()
            high, low = split(held[side, level])
            part_high[b, pl.ds(i * height, height)] = high
            part_low[b, pl.ds(i * height, height)] = low
        for column in range(0, keep, tile):
            image_columns(b, pl.ds(order + column, tile))

    def image_work(b, column):
        image_columns(b, pl.ds(column, tile))

    def second_work(b, column):
        weights = pl.ds(order + keep + column, tile)
        second[b, :, pl.ds(column, tile)] = product(part_high[b], part_low[b], weight_high[:, weights], weight_low[:, weights])

    unit = 0.75
    urgent.append((0.9, sketch_work))
    for i in range(order // batch):
        urgent.append((1.2, functools.partial(right_work, i)))
    for i in range(order // batch):
        urgent.append((0.5, functools.partial(left_work, i)))

    for b, arrivals in enumerate(pairs):
        for p in range(pieces):
            for m in arrivals:
                if m == 0:
                    continue
                ring_copy(m, p).wait_recv()
                for further in after(m):
                    start(ring_copy(further, p))
                start(pair_copy(m, p))
                if p == pieces - 1 and m == arrivals[-1] or m == chips // 2 and p == pieces - 1:
                    cross_start()
                    urgent.append((unit + 0.5, functools.partial(split_work, b)))
                    for column in range(0, order, tile):
                        later.append((unit, functools.partial(image_work, b, column)))
                    for column in range(0, keep, tile):
                        later.append((unit, functools.partial(second_work, b, column)))
                if m != chips // 2 or p < pieces - 1:
                    run(2.8 / pieces)
    while urgent:
        urgent.pop(0)[1]()

    choice_copy.wait_recv()

    def chosen(d, mine, there, shape):
        own = jnp.broadcast_to(choice_ref[0:1, 0:1], shape) == float(d)
        far = jnp.broadcast_to(choice_there[0:1, 0:1], shape) == float(d)
        return jnp.where(own, mine, 0.0) + jnp.where(far, there, 0.0)

    def half(m):
        return pl.ds(m * height, height)

    def term_copy(m):
        return remote(term_out.at[half(m)], term_in.at[half(m)], term_send.at[m], term_recv.at[m], sibling)

    def full_copy(m):
        return remote(left_full.at[pl.ds((chips + m) * height, height)], right_full.at[half(m)], full_send.at[m], full_recv.at[m], sibling)

    def halves(i, result):
        for k, m in enumerate(orders[i]):
            own = result[2 * k * height : (2 * k + 1) * height]
            yield m, own, (chips - m) % chips, result[(2 * k + 1) * height : (2 * k + 2) * height]

    def rows_of(i):
        return pl.ds(i * batch, batch)

    def term_work(i):
        for column in range(0, keep, tile):
            inner = pl.ds(order + column, tile)
            result = product(left_high[rows_of(i)], left_low[rows_of(i)], image_high[:, inner], image_low[:, inner])
            for m, own, there, far in halves(i, result):
                term[half(m), pl.ds(column, tile)] = own
                term_out[half(there), pl.ds(column, tile)] = far
        for m in orders[i]:
            start(term_copy((chips - m) % chips))

    def full_work(i, column):
        inner = pl.ds(column, tile)
        result = product(left_high[rows_of(i)], left_low[rows_of(i)], image_high[:, inner], image_low[:, inner])
        for m, own, there, far in halves(i, result):
            left_full[pl.ds(m * height, height), inner] = own
            left_full[pl.ds((chips + there) * height, height), inner] = far
        if column + tile == order:
            for m in orders[i]:
                full_copy((chips - m) % chips).start()

    done_terms = []
    for i in range(len(pairs)):
        urgent.append((unit + 0.1, lambda i=i: (term_work(i), done_terms.extend(orders[i]))))
    for i in range(len(pairs)):
        for column in range(0, order, tile):
            later.append((unit, functools.partial(full_work, i, column)))

    def sum_copy(m, d):
        device = ahead if m >= chips // 2 else behind
        return remote(outgoing.at[m - 1, d], incoming.at[m - 1, d], sum_send.at[m - 1, d], sum_recv.at[m - 1, d], device)

    shape = (height, keep)
    for r in range(chips // 2):
        steps = [(chips // 2 + r, chips // 2 + r - 1), (chips // 2 - 1 - r, chips // 2 - r)]
        for m, before in steps:
            if m == 0:
                continue
            while m not in done_terms:
                urgent.pop(0)[1]()
            term_copy(m).wait_recv()
            for d in range(reach):
                value = chosen(d, term[half(m)], term_in[half(m)], shape)
                if r > 0:
                    sum_copy(before, d).wait_recv()
                    value = value + incoming[before - 1, d]
                outgoing[m - 1, d] = value
                start(sum_copy(m, d))
                run(2.8 / reach)
        cross_start()
    while crossing:
        cross_start()
    while urgent or later:
        (urgent or later).pop(0)[1]()

    def mail_copy(d):
        return remote(mail_out.at[d - 1], mail_in.at[d - 1], mail_send.at[d - 1], mail_recv.at[d - 1], sector(d))

    def tile_copy(d):
        return remote(tile_out, tile_in.at[d - 1], tile_send.at[d - 1], tile_recv.at[d - 1], sector(d))

    term_copy(0).wait_recv()
    for d in reversed(range(reach)):
        value = chosen(d, term[half(0)], term_in[half(0)], shape)
        for before in (chips - 1, 1):
            sum_copy(before, d).wait_recv()
            value = value + incoming[before - 1, d]
        if d > 0:
            mail_out[d - 1] = value
            start(mail_copy(d))
        else:
            sums[0, 0, pl.ds(0, height)] = value

    small = (8, order)
    total = jnp.zeros(small, jnp.float32)
    for m in range(chips):
        full_copy(m).wait_recv()
        for d in range(1, reach):
            cross_copy(d, m).wait_recv()

        def add(i, carry, m=m):
            rows = pl.ds(pl.multiple_of(i * 8, 8), 8)
            for d in range(reach):
                state = held[0, m, rows] if d == 0 else other[d - 1, pl.ds(pl.multiple_of(m * height + i * 8, 8), 8)]
                carry = carry + state * chosen(d, left_full[pl.ds(pl.multiple_of(m * height + i * 8, 8), 8)], right_full[pl.ds(pl.multiple_of(m * height + i * 8, 8), 8)], small)
            return carry

        total = lax.fori_loop(0, height // 8, add, total)
    own = held[0, 0]
    up = jnp.broadcast_to(jnp.sum(total, keepdims=True), (8, keep))
    down = jnp.broadcast_to(jnp.sum(own * own, keepdims=True), (8, keep))
    row = lax.broadcasted_iota(jnp.int32, (8, keep), 0)
    tile_out[...] = jnp.where(row == 0, up, down)
    for m in range(chips):
        full_copy(m).wait_send()
    for d in range(1, sectors):
        start(tile_copy(d))
    for d in range(1, reach):
        mail_copy(d).wait_recv()
        sums[0, 0, pl.ds(0, height)] += mail_in[d - 1]
    both = tile_out[...]
    for d in range(1, sectors):
        tile_copy(d).wait_recv()
        both = both + tile_in[d - 1]
    sums[0, 0, pl.ds(height, 8)] = both

    spans = [pl.ds(p * part, part if p < pieces - 1 else part + 8) for p in range(pieces)]

    def again_copy(m, p):
        return onward(sums, m, spans[p], again_send.at[m - 1, p], again_recv.at[m - 1, p])

    def both_copy(m, p):
        return remote(sums.at[0, m, spans[p]], sums.at[1, m, spans[p]], both_send.at[m, p], both_recv.at[m, p], sibling)

    for arrivals in [(0,)] + pairs:
        for p in range(pieces):
            for m in arrivals:
                if m == 0 and len(arrivals) > 1:
                    continue
                if m > 0:
                    again_copy(m, p).wait_recv()
                for further in after(m):
                    start(again_copy(further, p))
                start(both_copy(m, p))
    for j in range(chips):
        for p in range(pieces):
            both_copy(j, p).wait_recv()

    both = jnp.zeros((8, keep), jnp.float32)
    for j in range(chips):
        for side in (0, 1):
            both = both + sums[side, j, pl.ds(height, 8)]
    energy = both[0:1] / both[1:2]
    at = {}
    energy_ref[...] = jnp.broadcast_to(energy, (8, keep))
    for b in range(chips // 2):
        for i, (side, m, slab) in enumerate(slabs_of(b)):
            rows = pl.ds(pl.multiple_of(slab * height, height), height)
            here = pl.ds(i * height, height)
            value = sums[side, m, pl.ds(0, height)] - energy * second[b, here]
            second[b, here] = value
            image_high[rows, pl.ds(0, keep)], image_low[rows, pl.ds(0, keep)] = split(value)
            at[side, m] = (b, here)
    for copy in started:
        copy.wait_send()
    started.clear()

    def far_copy(d, m):
        return remote(
            second.at[at[0, m]], rows_there(d, 0, m), far_send.at[d - 1, m], far_recv.at[d - 1, m], sector(sectors - d)
        )

    def row_there(side, m):
        return (2 * blocks.index(m) if side == 0 else 2 * blocks.index((chips - m) % chips) + 1) * height

    def rows_there(d, side, m):
        buffer = (left_full, right_full)[(d - 1) // 2]
        return buffer.at[pl.ds(row_there(side, m), height), pl.ds((d - 1) % 2 * keep, keep)]

    def near_copy(d, m):
        return remote(rows_there(d, 0, m), rows_there(d, 1, m), near_send.at[d - 1, m], near_recv.at[d - 1, m], sibling)

    for m in range(chips):
        for d in range(1, reach):
            start(far_copy(d, m))

    def picked(shape, options):
        flag = jnp.broadcast_to(choice_ref[0:1, 0:1], shape)
        result = options[0]
        for d in range(1, reach):
            result = jnp.where(flag == float(d), options[d], result)
        return result

    gram, inverse, strips = term, term_out, term_in
    for b in range(chips // 2):
        one = lax.dot_general(
            second[b], second[b], (((0,), (0,)), ((), ())), precision=EXACT, preferred_element_type=jnp.float32
        )
        gram[...] = one if b == 0 else gram[...] + one
    count = keep // BLOCK
    row = lax.broadcasted_iota(jnp.int32, (keep, keep), 0)
    column = lax.broadcasted_iota(jnp.int32, (keep, keep), 1)
    inverse[...] = jnp.where(row == column, 1.0, 0.0)
    tall_row = lax.broadcasted_iota(jnp.int32, (keep, BLOCK), 0)
    left_part = order // count

    def strip_copy(d, here, b):
        target = other.at[d - 1, here, pl.ds(0, keep)]
        return remote(strips.at[here], target, strip_send.at[d - 1, b], strip_recv.at[d - 1, b], sector(sectors - d))

    def pivot_copy(d, here, b):
        target = other.at[d - 1, here, pl.ds(keep, BLOCK)]
        return remote(pivot_out.at[here], target, pivot_send.at[d - 1, b], pivot_recv.at[d - 1, b], sector(sectors - d))

    def block_step(b, carry):
        begin = pl.multiple_of(b * BLOCK, BLOCK)
        here = pl.ds(begin, BLOCK)
        strips[here] = inverse[here]
        for d in range(1, reach):
            strip_copy(d, here, b).start()

        @pl.when(b == count - 1)
        def _():
            for d in range(1, reach):
                for m in range(chips):
                    far_copy(d, m).wait_recv()
                    near_copy(d, m).start()

        slice_ = pl.ds(pl.multiple_of(b * left_part, left_part), left_part)
        applied = product(left_high[slice_], left_low[slice_], image_high[:, pl.ds(0, keep)], image_low[:, pl.ds(0, keep)])
        image_high[slice_, pl.ds(2 * keep, keep)], image_low[slice_, pl.ds(2 * keep, keep)] = split(applied)
        pivot = invert_blocks([gram[here, here]])[0]
        pivot_out[here] = pivot
        for d in range(1, reach):
            pivot_copy(d, here, b).start()
        panel = jnp.where(tall_row >= begin + BLOCK, gram[:, here], 0.0)
        low = exact_nt(panel, pivot)
        strip = exact_nn(pivot, inverse[here, :])
        inverse[...] = inverse[...] - exact_nn(low, strip)
        inverse[here, :] = strip
        gram[...] = gram[...] - exact_nt(low, low)
        return carry

    lax.fori_loop(0, count, block_step, 0)

    for d in range(1, reach):
        for m in range(chips):
            near_copy(d, m).wait_recv()
    for side in (0, 1):
        for m in range(chips):
            rows = pl.ds(row_there(side, m), height)
            b, inner = at[side, m]
            options = [second[b, inner]] + [rows_there(d, side, m)[...] for d in range(1, reach)]
            high, low = split(picked((height, keep), options))
            image_high[rows, pl.ds(keep, keep)] = high
            image_low[rows, pl.ds(keep, keep)] = low

    def tall(buffer, k):
        return buffer[:, pl.ds(k * keep, keep)]

    middle = ((0,), (0,))
    unscaled = product(tall(image_high, 1), tall(image_low, 1), tall(image_high, 2), tall(image_low, 2), middle)
    own_high, own_low = split(inverse[...])
    across = ((1,), (1,))
    high, low = split(unscaled)
    mid_high[...], mid_low[...] = split(product(high, low, own_high, own_low, across))
    slab_high, slab_low = split(second[at[0, 0]])
    basis_ref[...] = product(slab_high, slab_low, own_high, own_low, across)
    for b in range(count):
        here = pl.ds(b * BLOCK, BLOCK)
        for d in range(1, reach):
            strip_copy(d, here, b).wait_recv()
        options = [strips[here]] + [other[d - 1, here, pl.ds(0, keep)] for d in range(1, reach)]
        high, low = split(picked((BLOCK, keep), options))
        right_high, right_low = split(product(high, low, mid_high[...], mid_low[...]))
        for d in range(1, reach):
            pivot_copy(d, here, b).wait_recv()
        options = [pivot_out[here]] + [other[d - 1, here, pl.ds(keep, BLOCK)] for d in range(1, reach)]
        high, low = split(picked((BLOCK, BLOCK), options))
        rotated_ref[here, :] = product(high, low, right_high, right_low)
    for copy in started:
        copy.wait_send()
    for d in range(1, reach):
        for m in range(chips):
            near_copy(d, m).wait_send()
        for b in range(count):
            here = pl.ds(b * BLOCK, BLOCK)
            strip_copy(d, here, b).wait_send()
            pivot_copy(d, here, b).wait_send()


def front(left_op, right_op, slab, sketch, choice):
    height, order = slab.shape
    keep = sketch.shape[1]
    sectors = lax.axis_size("sec")
    chips = lax.axis_size("op") // 2
    reach = min(4, sectors)
    pieces = 2
    wide, half = jnp.float32, jnp.bfloat16
    columns = order + keep
    batch = 4 * height
    dma = pltpu.SemaphoreType.DMA
    scratch = [
        ((2, chips, height, order), wide), ((reach - 1, chips * height, order), wide), ((order, order), wide),
        ((order, order), wide), ((order, keep), wide), ((order, order), half), ((order, order), half),
        ((order, columns + keep), half), ((order, columns + keep), half),
        ((chips // 2, batch, order), half), ((chips // 2, batch, order), half), ((order, columns), half), ((order, columns), half),
        ((chips // 2, batch, keep), wide), ((chips * height, keep), wide), ((chips * height, keep), wide),
        ((chips * height, keep), wide), ((chips - 1, reach, height, keep), wide), ((chips - 1, reach, height, keep), wide),
        ((reach - 1, height, keep), wide), ((reach - 1, height, keep), wide), ((8, keep), wide), ((sectors - 1, 8, keep), wide),
        ((2, chips, height + 8, keep), wide), ((8, 128), wide), ((keep, BLOCK), wide), ((keep, keep), half), ((keep, keep), half),
    ]
    counts = [
        (4,), (2,), (chips - 1, pieces), (chips - 1, pieces), (chips, pieces), (chips, pieces), (reach - 1, chips),
        (reach - 1, chips), (chips,), (chips,), (chips - 1, reach), (chips - 1, reach), (chips,), (chips,), (reach - 1,),
        (reach - 1,), (sectors - 1,), (sectors - 1,), (chips - 1, pieces), (chips - 1, pieces), (chips, pieces), (chips, pieces),
        (reach - 1, chips), (reach - 1, chips), (reach - 1, chips), (reach - 1, chips), (reach - 1, keep // BLOCK),
        (reach - 1, keep // BLOCK), (reach - 1, keep // BLOCK), (reach - 1, keep // BLOCK),
    ]
    anywhere = pl.BlockSpec(memory_space=pl.ANY)
    inside = pl.BlockSpec(memory_space=pltpu.VMEM)
    sizes = (chips, sectors, reach, height, order, keep, pieces)
    return pl.pallas_call(
        functools.partial(front_kernel, sizes),
        out_shape=tuple(jax.ShapeDtypeStruct((rows, keep), wide) for rows in (keep, height, 8)),
        in_specs=[anywhere] * 4 + [inside],
        out_specs=(inside, inside, inside),
        scratch_shapes=[pltpu.VMEM(shape, kind) for shape, kind in scratch] + [dma(count) for count in counts],
        compiler_params=pltpu.CompilerParams(collective_id=0, has_side_effects=True, vmem_limit_bytes=61 * 2**20),
        cost_estimate=pl.CostEstimate(flops=24 * order**3, bytes_accessed=48 * order**2, transcendentals=0),
        name="front",
    )(left_op, right_op, slab, sketch, choice)


def body(left_ops, right_ops, amplitudes, sketch, sector_shift):
    left_op = left_ops[0, 0]
    sectors = lax.axis_size("sec")
    height = amplitudes.shape[1]
    choice = lax.rem(sector_shift[0], sectors)
    flag = jnp.full((8, 128), choice.astype(jnp.float32))
    rotated, basis_slab, quotient = front(left_op, right_ops[0, 0], amplitudes[0], sketch, flag)
    return (rotated[None, None], basis_slab[None], quotient[0, 0])


def solution(mesh):
    in_specs = (
        P("op", "sec", None, None),
        P("op", "sec", None, None),
        P("sec", "op", None),
        P(),
        P("op"),
    )
    out_specs = (P("op", "sec", None, None), P("sec", "op", None), P())
    return jax.shard_map(body, mesh=mesh, in_specs=in_specs, out_specs=out_specs, check_vma=False)
```

```python
import functools

import jax
import jax.numpy as jnp
from jax import lax
from jax.experimental import pallas as pl
from jax.experimental.pallas import tpu as pltpu
from jax.sharding import PartitionSpec as P

HALF = 64
BLOCK = 128


def thirds(value):
    high = value.astype(jnp.bfloat16)
    rest = value - high.astype(jnp.float32)
    middle = rest.astype(jnp.bfloat16)
    return high, middle, (rest - middle.astype(jnp.float32)).astype(jnp.bfloat16)


def exact(first, second, axis):
    high, middle, low = thirds(first)
    other_high, other_middle, other_low = thirds(second)
    left = jnp.concatenate([high, high, middle, middle, high, low], axis=1)
    right = jnp.concatenate([other_high, other_middle, other_high, other_middle, other_low, other_high], axis=axis)
    return lax.dot_general(left, right, (((1,), (axis,)), ((), ())), preferred_element_type=jnp.float32)


def exact_nn(first, second):
    return exact(first, second, 0)


def exact_nt(first, second):
    return exact(first, second, 1)


def eliminate_many(blocks):
    sub = lax.broadcasted_iota(jnp.int32, (8, BLOCK), 0)
    lane = lax.broadcasted_iota(jnp.int32, (8, BLOCK), 1)
    rows = [[block[8 * c : 8 * c + 8, :] for c in range(HALF // 8)] for block in blocks]
    for j in range(0, HALF, 2):
        home = j // 8
        for chunk in rows:
            row = chunk[home][j % 8 : j % 8 + 1, :]
            follower = chunk[home][j % 8 + 1 : j % 8 + 2, :]
            head = jnp.broadcast_to(row[:, j : j + 1], (1, BLOCK))
            cross = jnp.broadcast_to(row[:, j + 1 : j + 2], (1, BLOCK))
            tail = jnp.broadcast_to(follower[:, j + 1 : j + 2], (1, BLOCK))
            head_inverse = 1.0 / head
            ratio = cross * head_inverse
            scaled = row * head_inverse
            reduced = follower - cross * scaled
            reduced_scaled = reduced * (head / (head * tail - cross * cross))
            for c in range(home, HALF // 8):
                column = jnp.broadcast_to(chunk[c][:, j : j + 1], (8, BLOCK))
                beside = jnp.broadcast_to(chunk[c][:, j + 1 : j + 2], (8, BLOCK)) - column * ratio
                if c == home:
                    column = jnp.where(sub > j % 8, column, 0.0)
                    beside = jnp.where(sub > j % 8 + 1, beside, 0.0)
                chunk[c] = chunk[c] - column * scaled - beside * reduced_scaled
    results = []
    for chunk in rows:
        scaled_chunks = []
        for c in range(HALF // 8):
            pivot = jnp.sum(jnp.where(lane == sub + 8 * c, chunk[c], 0.0), axis=1, keepdims=True)
            scaled_chunks.append(jnp.where(lane >= HALF, chunk[c] * lax.rsqrt(pivot), 0.0))
        results.append(jnp.concatenate(scaled_chunks, axis=0))
    return results


def invert_blocks(blocks):
    lane = lax.broadcasted_iota(jnp.int32, (HALF, BLOCK), 1)
    row = lax.broadcasted_iota(jnp.int32, (HALF, BLOCK), 0)
    unit = jnp.where(lane == row + HALF, 1.0, 0.0)
    empty = jnp.zeros((HALF, BLOCK), jnp.float32)

    def tall(top):
        return jnp.concatenate([top, empty], axis=0)

    first = eliminate_many([jnp.where(lane < HALF, block[:HALF], unit) for block in blocks])
    upper = [pltpu.roll(one, HALF, 1) for one in first]
    lower = [block[HALF:] for block in blocks]
    coupling = [exact_nt(low, tall(up)) for low, up in zip(lower, upper)]
    schur = [pltpu.roll(low, HALF, 1) - exact_nt(mid, tall(mid)) for low, mid in zip(lower, coupling)]
    second = eliminate_many([jnp.where(lane < HALF, one, unit) for one in schur])
    result = []
    for up, mid, right in zip(upper, coupling, second):
        carried = exact_nn(mid, tall(up))
        left = exact_nn(pltpu.roll(right, HALF, 1), tall(carried))
        result.append(jnp.concatenate([up, right - left], axis=0))
    return result


def split(value):
    high = value.astype(jnp.bfloat16)
    return high, (value - high.astype(jnp.float32)).astype(jnp.bfloat16)


def product(high, low, other_high, other_low, contract=((1,), (0,))):
    def one(first, second):
        return lax.dot_general(first, second, (contract, ((), ())), preferred_element_type=jnp.float32)

    return one(high, other_high) + (one(high, other_low) + one(low, other_high))


def ring_chip(position, chips):
    return 2 * position + lax.div(position, chips // 2) * (2 * chips - 1 - 4 * position)


def front_kernel(
    sizes, left_ref, right_ref, slab_ref, sketch_ref, choice_ref,
    rotated_ref, basis_ref, energy_ref,
    held, other, left_full, right_full, sketch_full, left_high, left_low, weight_high, weight_low,
    part_high, part_low, image_high, image_low, second, term, term_out, term_in, outgoing, incoming,
    mail_out, mail_in, tile_out, tile_in, sums, choice_there, pivot_out, pivot_in, mid_high, mid_low,
    local_sem, choice_sem, ring_send, ring_recv, pair_send, pair_recv, cross_send, cross_recv, term_send, term_recv,
    sum_send, sum_recv, full_send, full_recv, mail_send, mail_recv, tile_send, tile_recv,
    again_send, again_recv, both_send, both_recv, far_send, far_recv, near_send, near_recv, strip_send, strip_recv, pivot_send,
    pivot_recv,
):
    chips, sectors, reach, height, order, keep, pieces = sizes
    op = lax.axis_index("op")
    sec = lax.axis_index("sec")
    core = lax.rem(op, 2)
    chip = lax.div(op, 2)
    lower = lax.div(chip, 2)
    position = lower + lax.rem(chip, 2) * (chips - 1 - 2 * lower)
    way = 1 - 2 * core

    def chip_at(steps, turn):
        return ring_chip(lax.rem(position + chips + turn * steps, chips), chips)

    ahead = {"op": 2 * chip_at(1, way) + core, "sec": sec}
    behind = {"op": 2 * chip_at(1, -way) + core, "sec": sec}
    sibling = {"op": 2 * chip + 1 - core, "sec": sec}

    def sector(distance):
        return {"op": op, "sec": lax.rem(sec + distance, sectors)}

    def remote(source, target, send, recv, device):
        return pltpu.make_async_remote_copy(
            src_ref=source, dst_ref=target, send_sem=send, recv_sem=recv, device_id=device, device_id_type=pl.DeviceIdType.MESH
        )

    started = []

    def start(copy):
        copy.start()
        started.append(copy)

    pairs = [(m, chips - m) for m in range(1, chips // 2)] + [(chips // 2, 0)]
    orders = pairs[::-1]
    blocks = [m for pair in orders for m in pair]
    copies = [
        pltpu.make_async_copy(slab_ref, held.at[0, pl.ds(0, height)], local_sem.at[0]),
        pltpu.make_async_copy(sketch_ref, sketch_full, local_sem.at[1]),
        pltpu.make_async_copy(right_ref, right_full, local_sem.at[2]),
    ]
    for copy in copies:
        copy.start()
    for place, m in enumerate(blocks):
        base = chip_at(m, -way) * 2 * height
        for side in (0, 1):
            begin = pl.multiple_of(base + (core if side == 0 else 1 - core) * height, height)
            pltpu.make_async_copy(
                left_ref.at[pl.ds(begin, height)], left_full.at[pl.ds((2 * place + side) * height, height)], local_sem.at[3]
            ).start()

    barrier = pltpu.get_barrier_semaphore()
    greeted = [ahead, behind, sibling] + [sector(d) for d in range(1, sectors)]
    for device in greeted:
        pl.semaphore_signal(barrier, inc=1, device_id=device, device_id_type=pl.DeviceIdType.MESH)
    pl.semaphore_wait(barrier, len(greeted))

    part = height // pieces

    def onward(view, m, send, recv):
        source, device = (m - 1, ahead) if m <= chips // 2 else ((m + 1) % chips, behind)
        return remote(view(source), view(m), send, recv, device)

    def after(m):
        if m == 0:
            return [1, chips - 1]
        if m < chips // 2:
            return [m + 1]
        return [m - 1] if m > chips // 2 + 1 else []

    def ring_copy(m, p):
        return onward(lambda i: held.at[0, pl.ds(i * height + p * part, part)], m, ring_send.at[m - 1, p], ring_recv.at[m - 1, p])

    def pair_copy(m, p):
        rows = pl.ds(m * height + p * part, part)
        return remote(held.at[0, rows], held.at[1, rows], pair_send.at[m, p], pair_recv.at[m, p], sibling)

    def cross_copy(d, j):
        return remote(
            held.at[0, pl.ds(j * height, height)], other.at[d - 1, pl.ds(j * height, height)], cross_send.at[d - 1, j], cross_recv.at[d - 1, j], sector(sectors - d)
        )

    crossing = [0] + [m for pair in pairs[:-1] for m in pair] + [chips // 2]

    def cross_start():
        if crossing:
            m = crossing.pop(0)
            for d in range(1, reach):
                start(cross_copy(d, m))

    copies[0].wait()
    for p in range(pieces):
        for m in after(0):
            start(ring_copy(m, p))
        start(pair_copy(0, p))
    choice_copy = remote(choice_ref, choice_there, choice_sem.at[0], choice_sem.at[1], sibling)
    start(choice_copy)
    cross_start()

    batch = 4 * height
    tile = min(512, keep)
    urgent, later = [], []

    def run(budget):
        while budget > 0 and (urgent or later):
            cost, work = (urgent or later).pop(0)
            work()
            budget -= cost

    def split_rows(source, high, low, first, count, columns):
        step = 32

        def one(i, carry):
            rows = pl.ds(pl.multiple_of(first + i * step, step), step)
            high[rows, columns], low[rows, columns] = split(source[rows, :])
            return carry

        lax.fori_loop(0, count // step, one, 0)

    def sketch_work():
        copies[1].wait()
        split_rows(sketch_full, weight_high, weight_low, 0, order, pl.ds(order + keep, keep))

    def right_work(i):
        if i == 0:
            copies[2].wait()
        split_rows(right_full, weight_high, weight_low, i * batch, batch, pl.ds(0, order))
        rows = pl.ds(i * batch, batch)
        inner = pl.ds(0, order)
        last = pl.ds(order + keep, keep)
        high, low = split(product(weight_high[rows, inner], weight_low[rows, inner], weight_high[:, last], weight_low[:, last]))
        weight_high[rows, pl.ds(order, keep)] = high
        weight_low[rows, pl.ds(order, keep)] = low

    def left_work(i):
        if i == 0:
            pltpu.make_async_copy(left_ref, left_full, local_sem.at[3]).wait()
        split_rows(left_full, left_high, left_low, i * batch, batch, pl.ds(0, order))

    def slabs_of(b):
        for m in pairs[b]:
            yield 0, m, chip_at(m, -way) * 2 + core
            yield 1, m, chip_at(m, way) * 2 + 1 - core

    def image_columns(b, columns):
        result = product(part_high[b], part_low[b], weight_high[:, columns], weight_low[:, columns])
        high, low = split(result)
        for i, (_, _, slab) in enumerate(slabs_of(b)):
            rows = pl.ds(pl.multiple_of(slab * height, height), height)
            image_high[rows, columns] = high[i * height : (i + 1) * height]
            image_low[rows, columns] = low[i * height : (i + 1) * height]

    def split_work(b):
        for i, (side, level, _) in enumerate(slabs_of(b)):
            if side == 1:
                for p in range(pieces):
                    pair_copy(level, p).wait_recv()
            high, low = split(held[side, pl.ds(level * height, height)])
            part_high[b, pl.ds(i * height, height)] = high
            part_low[b, pl.ds(i * height, height)] = low
        for column in range(0, keep, tile):
            image_columns(b, pl.ds(order + column, tile))

    def image_work(b, column):
        image_columns(b, pl.ds(column, tile))

    def second_work(b, column):
        weights = pl.ds(order + keep + column, tile)
        second[b, :, pl.ds(column, tile)] = product(part_high[b], part_low[b], weight_high[:, weights], weight_low[:, weights])

    unit = 0.75
    urgent.append((0.9, sketch_work))
    for i in range(order // batch):
        urgent.append((1.2, functools.partial(right_work, i)))
    for i in range(order // batch):
        urgent.append((0.5, functools.partial(left_work, i)))

    for b, arrivals in enumerate(pairs):
        for p in range(pieces):
            for m in arrivals:
                if m == 0:
                    continue
                ring_copy(m, p).wait_recv()
                for further in after(m):
                    start(ring_copy(further, p))
                start(pair_copy(m, p))
                if p == pieces - 1 and m == arrivals[-1] or m == chips // 2 and p == pieces - 1:
                    cross_start()
                    urgent.append((unit + 0.5, functools.partial(split_work, b)))
                    for column in range(0, order, tile):
                        later.append((unit, functools.partial(image_work, b, column)))
                    for column in range(0, keep, tile):
                        later.append((unit, functools.partial(second_work, b, column)))
                if m != chips // 2 or p < pieces - 1:
                    run(2.8 / pieces)
    while urgent:
        urgent.pop(0)[1]()

    choice_copy.wait_recv()

    def chosen(d, mine, there, shape):
        own = jnp.broadcast_to(choice_ref[0:1, 0:1], shape) == float(d)
        far = jnp.broadcast_to(choice_there[0:1, 0:1], shape) == float(d)
        return jnp.where(own, mine, 0.0) + jnp.where(far, there, 0.0)

    def half(m):
        return pl.ds(m * height, height)

    def term_copy(m):
        return remote(term_out.at[half(m)], term_in.at[half(m)], term_send.at[m], term_recv.at[m], sibling)

    def full_copy(m):
        return remote(left_full.at[pl.ds((chips + m) * height, height)], right_full.at[half(m)], full_send.at[m], full_recv.at[m], sibling)

    def halves(i, result):
        for k, m in enumerate(orders[i]):
            own = result[2 * k * height : (2 * k + 1) * height]
            yield m, own, (chips - m) % chips, result[(2 * k + 1) * height : (2 * k + 2) * height]

    def rows_of(i):
        return pl.ds(i * batch, batch)

    def term_work(i):
        for column in range(0, keep, tile):
            inner = pl.ds(order + column, tile)
            result = product(left_high[rows_of(i)], left_low[rows_of(i)], image_high[:, inner], image_low[:, inner])
            for m, own, there, far in halves(i, result):
                term[half(m), pl.ds(column, tile)] = own
                term_out[half(there), pl.ds(column, tile)] = far
        for m in orders[i]:
            term_copy((chips - m) % chips).start()

    def full_work(i, column):
        inner = pl.ds(column, tile)
        result = product(left_high[rows_of(i)], left_low[rows_of(i)], image_high[:, inner], image_low[:, inner])
        for m, own, there, far in halves(i, result):
            left_full[pl.ds(m * height, height), inner] = own
            left_full[pl.ds((chips + there) * height, height), inner] = far
        if column + tile == order:
            for m in orders[i]:
                full_copy((chips - m) % chips).start()

    done_terms = []
    for i in range(len(pairs)):
        urgent.append((unit + 0.1, lambda i=i: (term_work(i), done_terms.extend(orders[i]))))
    for i in range(len(pairs)):
        for column in range(0, order, tile):
            later.append((unit, functools.partial(full_work, i, column)))

    def sum_copy(m, d):
        device = ahead if m >= chips // 2 else behind
        return remote(outgoing.at[m - 1, d], incoming.at[m - 1, d], sum_send.at[m - 1, d], sum_recv.at[m - 1, d], device)

    shape = (height, keep)
    for r in range(chips // 2):
        steps = [(chips // 2 + r, chips // 2 + r - 1), (chips // 2 - 1 - r, chips // 2 - r)]
        for m, before in steps:
            if m == 0:
                continue
            while m not in done_terms:
                urgent.pop(0)[1]()
            term_copy(m).wait_recv()
            for d in range(reach):
                value = chosen(d, term[half(m)], term_in[half(m)], shape)
                if r > 0:
                    sum_copy(before, d).wait_recv()
                    value = value + incoming[before - 1, d]
                outgoing[m - 1, d] = value
                start(sum_copy(m, d))
                run(2.8 / reach)
        cross_start()
    while crossing:
        cross_start()
    while urgent or later:
        (urgent or later).pop(0)[1]()

    def mail_copy(d):
        return remote(mail_out.at[d - 1], mail_in.at[d - 1], mail_send.at[d - 1], mail_recv.at[d - 1], sector(d))

    def tile_copy(d):
        return remote(tile_out, tile_in.at[d - 1], tile_send.at[d - 1], tile_recv.at[d - 1], sector(d))

    term_copy(0).wait_recv()
    for d in reversed(range(reach)):
        value = chosen(d, term[half(0)], term_in[half(0)], shape)
        for before in (chips - 1, 1):
            sum_copy(before, d).wait_recv()
            value = value + incoming[before - 1, d]
        if d > 0:
            mail_out[d - 1] = value
            start(mail_copy(d))
        else:
            sums[0, 0, pl.ds(0, height)] = value

    small = (8, order)
    total = jnp.zeros(small, jnp.float32)
    for m in range(chips):
        full_copy(m).wait_recv()
        for d in range(1, reach):
            cross_copy(d, m).wait_recv()

        def add(i, carry, m=m):
            rows = pl.ds(pl.multiple_of(m * height + i * 8, 8), 8)
            for d in range(reach):
                state = held[0, rows] if d == 0 else other[d - 1, rows]
                carry = carry + state * chosen(d, left_full[rows], right_full[rows], small)
            return carry

        total = lax.fori_loop(0, height // 8, add, total)
    own = held[0, pl.ds(0, height)]
    up = jnp.broadcast_to(jnp.sum(total, keepdims=True), (8, keep))
    down = jnp.broadcast_to(jnp.sum(own * own, keepdims=True), (8, keep))
    row = lax.broadcasted_iota(jnp.int32, (8, keep), 0)
    tile_out[...] = jnp.where(row == 0, up, down)
    for m in range(chips):
        full_copy(m).wait_send()
    for copy in started[: len(started) - (reach - 1)]:
        copy.wait_send()
    del started[: len(started) - (reach - 1)]
    for d in range(1, sectors):
        start(tile_copy(d))
    for d in range(1, reach):
        mail_copy(d).wait_recv()
        sums[0, 0, pl.ds(0, height)] += mail_in[d - 1]
    both = tile_out[...]
    for d in range(1, sectors):
        tile_copy(d).wait_recv()
        both = both + tile_in[d - 1]
    sums[0, 0, pl.ds(height, 8)] = both

    spans = [pl.ds(p * part, part if p < pieces - 1 else part + 8) for p in range(pieces)]

    def again_copy(m, p):
        return onward(lambda i: sums.at[0, i, spans[p]], m, again_send.at[m - 1, p], again_recv.at[m - 1, p])

    def both_copy(m, p):
        return remote(sums.at[0, m, spans[p]], sums.at[1, m, spans[p]], both_send.at[m, p], both_recv.at[m, p], sibling)

    def row_there(side, m):
        return (2 * blocks.index(m) if side == 0 else 2 * blocks.index((chips - m) % chips) + 1) * height

    def rows_there(d, side, m):
        buffer = (left_full, right_full)[(d - 1) // 2]
        return buffer.at[pl.ds(row_there(side, m), height), pl.ds((d - 1) % 2 * keep, keep)]

    def far_copy(d, m):
        source = sums.at[0, m, pl.ds(0, height)]
        return remote(source, rows_there(d, 0, m), far_send.at[d - 1, m], far_recv.at[d - 1, m], sector(sectors - d))

    def near_copy(d, m):
        return remote(rows_there(d, 0, m), rows_there(d, 1, m), near_send.at[d - 1, m], near_recv.at[d - 1, m], sibling)

    def second_there(d, m):
        place = (d - 1) * chips + m
        return incoming.at[place // reach, place % reach]

    def other_work(d, first):
        rows = pl.ds(first * height, batch)
        high, low = split(other[d - 1, rows])
        part_high[0], part_low[0] = high, low
        for column in range(0, keep, tile):
            weights = pl.ds(order + keep + column, tile)
            result = product(part_high[0], part_low[0], weight_high[:, weights], weight_low[:, weights])
            for i in range(4):
                second_there(d, first + i)[:, pl.ds(column, tile)] = result[i * height : (i + 1) * height]

    for d in range(1, reach):
        for first in range(0, chips, 4):
            later.append((unit + 0.5, functools.partial(other_work, d, first)))
    for arrivals in [(0,)] + pairs:
        for p in range(pieces):
            for m in arrivals:
                if m == 0 and len(arrivals) > 1:
                    continue
                if m > 0:
                    again_copy(m, p).wait_recv()
                for further in after(m):
                    start(again_copy(further, p))
                start(both_copy(m, p))
                if p == pieces - 1:
                    for d in range(1, reach):
                        start(far_copy(d, m))
                run(0.1)
    while later:
        later.pop(0)[1]()
    for j in range(chips):
        for p in range(pieces):
            both_copy(j, p).wait_recv()

    both = jnp.zeros((8, keep), jnp.float32)
    for j in range(chips):
        for side in (0, 1):
            both = both + sums[side, j, pl.ds(height, 8)]
    energy = both[0:1] / both[1:2]
    at = {}
    energy_ref[...] = jnp.broadcast_to(energy, (8, keep))
    for b in range(chips // 2):
        for i, (side, m, slab) in enumerate(slabs_of(b)):
            rows = pl.ds(pl.multiple_of(slab * height, height), height)
            here = pl.ds(i * height, height)
            value = sums[side, m, pl.ds(0, height)] - energy * second[b, here]
            second[b, here] = value
            image_high[rows, pl.ds(0, keep)], image_low[rows, pl.ds(0, keep)] = split(value)
            at[side, m] = (b, here)
    for m in range(chips):
        term_copy(m).wait_send()

    def picked(shape, options):
        flag = jnp.broadcast_to(choice_ref[0:1, 0:1], shape)
        result = options[0]
        for d in range(1, reach):
            result = jnp.where(flag == float(d), options[d], result)
        return result

    gram, inverse, strips = term, term_out, term_in
    for b in range(chips // 2):
        one = exact_nn(second[b].T, second[b])
        gram[...] = one if b == 0 else gram[...] + one
    count = keep // BLOCK
    row = lax.broadcasted_iota(jnp.int32, (keep, keep), 0)
    column = lax.broadcasted_iota(jnp.int32, (keep, keep), 1)
    inverse[...] = jnp.where(row == column, 1.0, 0.0)
    left_part = order // count

    def strip_there(d, b):
        return held.at[(d - 1) // 2, pl.ds(b * BLOCK, BLOCK), pl.ds((d - 1) % 2 * keep, (b + 1) * BLOCK)]

    def strip_copy(d, b):
        source = strips.at[pl.ds(b * BLOCK, BLOCK), pl.ds(0, (b + 1) * BLOCK)]
        return remote(source, strip_there(d, b), strip_send.at[d - 1, b], strip_recv.at[d - 1, b], sector(sectors - d))

    def pivot_copy(d, b):
        here = pl.ds(b * BLOCK, BLOCK)
        return remote(pivot_out.at[here], pivot_in.at[d - 1, here], pivot_send.at[d - 1, b], pivot_recv.at[d - 1, b], sector(sectors - d))

    for b in range(count):
        here = pl.ds(b * BLOCK, BLOCK)
        upto = pl.ds(0, (b + 1) * BLOCK)
        below = pl.ds((b + 1) * BLOCK, keep - (b + 1) * BLOCK)
        strips[here, upto] = inverse[here, upto]
        for d in range(1, reach):
            start(strip_copy(d, b))
        if b == count // 2:
            for d in range(1, reach):
                for m in range(chips):
                    far_copy(d, m).wait_recv()
                    rows_there(d, 0, m)[...] = rows_there(d, 0, m)[...] - energy * second_there(d, m)[...]
                    start(near_copy(d, m))
        slice_ = pl.ds(b * left_part, left_part)
        applied = product(left_high[slice_], left_low[slice_], image_high[:, pl.ds(0, keep)], image_low[:, pl.ds(0, keep)])
        image_high[slice_, pl.ds(2 * keep, keep)], image_low[slice_, pl.ds(2 * keep, keep)] = split(applied)
        pivot = invert_blocks([gram[here, here]])[0]
        pivot_out[here] = pivot
        for d in range(1, reach):
            start(pivot_copy(d, b))
        strip = exact_nn(pivot, strips[here, upto])
        inverse[here, upto] = strip
        if b < count - 1:
            low = exact_nt(gram[below, here], pivot)
            gram[below, below] = gram[below, below] - exact_nt(low, low)
            inverse[below, upto] = inverse[below, upto] - exact_nn(low, strip)

    for d in range(1, reach):
        for m in range(chips):
            near_copy(d, m).wait_recv()
    step = max(1, BLOCK // (2 * height))
    for first in range(0, chips, step):
        values = []
        for m in blocks[first : first + step]:
            for side, mine in ((0, m), (1, (chips - m) % chips)):
                b, inner = at[side, mine]
                options = [second[b, inner]] + [rows_there(d, side, mine)[...] for d in range(1, reach)]
                values.append(picked((height, keep), options))
        high, low = split(jnp.concatenate(values, axis=0).T)
        place = pl.ds(first * 2 * height, step * 2 * height)
        for i in range(keep // batch):
            part_high[i, :, place] = high[i * batch : (i + 1) * batch]
            part_low[i, :, place] = low[i * batch : (i + 1) * batch]

    own_high, own_low = split(inverse[...])
    across = ((1,), (1,))
    after_left = pl.ds(2 * keep, keep)
    for i in range(keep // batch):
        high, low = split(product(part_high[i], part_low[i], image_high[:, after_left], image_low[:, after_left]))
        mid_high[rows_of(i)], mid_low[rows_of(i)] = split(product(high, low, own_high, own_low, across))
    slab_high, slab_low = split(second[at[0, 0]])
    basis_ref[...] = product(slab_high, slab_low, own_high, own_low, across)
    for b in range(count):
        here = pl.ds(b * BLOCK, BLOCK)
        upto = pl.ds(0, (b + 1) * BLOCK)
        for d in range(1, reach):
            strip_copy(d, b).wait_recv()
        options = [strips[here, upto]] + [strip_there(d, b)[...] for d in range(1, reach)]
        high, low = split(picked((BLOCK, (b + 1) * BLOCK), options))
        right_high, right_low = split(product(high, low, mid_high[upto, :], mid_low[upto, :]))
        for d in range(1, reach):
            pivot_copy(d, b).wait_recv()
        options = [pivot_out[here]] + [pivot_in[d - 1, here] for d in range(1, reach)]
        high, low = split(picked((BLOCK, BLOCK), options))
        rotated_ref[here, :] = product(high, low, right_high, right_low)
    for copy in started:
        copy.wait_send()


def front(left_op, right_op, slab, sketch, choice):
    height, order = slab.shape
    keep = sketch.shape[1]
    sectors = lax.axis_size("sec")
    chips = lax.axis_size("op") // 2
    reach = min(4, sectors)
    pieces = 2
    wide, half = jnp.float32, jnp.bfloat16
    columns = order + keep
    batch = 4 * height
    dma = pltpu.SemaphoreType.DMA
    scratch = [
        ((2, chips * height, order), wide), ((reach - 1, chips * height, order), wide), ((order, order), wide),
        ((order, order), wide), ((order, keep), wide), ((order, order), half), ((order, order), half),
        ((order, columns + keep), half), ((order, columns + keep), half),
        ((chips // 2, batch, order), half), ((chips // 2, batch, order), half), ((order, columns), half), ((order, columns), half),
        ((chips // 2, batch, keep), wide), ((chips * height, keep), wide), ((chips * height, keep), wide),
        ((chips * height, keep), wide), ((chips - 1, reach, height, keep), wide), ((chips - 1, reach, height, keep), wide),
        ((reach - 1, height, keep), wide), ((reach - 1, height, keep), wide), ((8, keep), wide), ((sectors - 1, 8, keep), wide),
        ((2, chips, height + 8, keep), wide), ((8, 128), wide), ((keep, BLOCK), wide), ((reach - 1, keep, BLOCK), wide), ((keep, keep), half), ((keep, keep), half),
    ]
    counts = [
        (4,), (2,), (chips - 1, pieces), (chips - 1, pieces), (chips, pieces), (chips, pieces), (reach - 1, chips),
        (reach - 1, chips), (chips,), (chips,), (chips - 1, reach), (chips - 1, reach), (chips,), (chips,), (reach - 1,),
        (reach - 1,), (sectors - 1,), (sectors - 1,), (chips - 1, pieces), (chips - 1, pieces), (chips, pieces), (chips, pieces),
        (reach - 1, chips), (reach - 1, chips), (reach - 1, chips), (reach - 1, chips), (reach - 1, keep // BLOCK),
        (reach - 1, keep // BLOCK), (reach - 1, keep // BLOCK), (reach - 1, keep // BLOCK),
    ]
    anywhere = pl.BlockSpec(memory_space=pl.ANY)
    inside = pl.BlockSpec(memory_space=pltpu.VMEM)
    sizes = (chips, sectors, reach, height, order, keep, pieces)
    return pl.pallas_call(
        functools.partial(front_kernel, sizes),
        out_shape=tuple(jax.ShapeDtypeStruct((rows, keep), wide) for rows in (keep, height, 8)),
        in_specs=[anywhere] * 4 + [inside],
        out_specs=(inside, inside, inside),
        scratch_shapes=[pltpu.VMEM(shape, kind) for shape, kind in scratch] + [dma(count) for count in counts],
        compiler_params=pltpu.CompilerParams(collective_id=0, has_side_effects=True, vmem_limit_bytes=63 * 2**20),
        cost_estimate=pl.CostEstimate(flops=24 * order**3, bytes_accessed=48 * order**2, transcendentals=0),
        name="front",
    )(left_op, right_op, slab, sketch, choice)


def body(left_ops, right_ops, amplitudes, sketch, sector_shift):
    left_op = left_ops[0, 0]
    sectors = lax.axis_size("sec")
    height = amplitudes.shape[1]
    choice = lax.rem(sector_shift[0], sectors)
    flag = jnp.full((8, 128), choice.astype(jnp.float32))
    rotated, basis_slab, quotient = front(left_op, right_ops[0, 0], amplitudes[0], sketch, flag)
    return (rotated[None, None], basis_slab[None], quotient[0, 0])


def solution(mesh):
    in_specs = (
        P("op", "sec", None, None),
        P("op", "sec", None, None),
        P("sec", "op", None),
        P(),
        P("op"),
    )
    out_specs = (P("op", "sec", None, None), P("sec", "op", None), P())
    return jax.shard_map(body, mesh=mesh, in_specs=in_specs, out_specs=out_specs, check_vma=False)
```

```python
import functools

import jax
import jax.numpy as jnp
from jax import lax
from jax.experimental import pallas as pl
from jax.experimental.pallas import tpu as pltpu
from jax.sharding import PartitionSpec as P

HALF = 64
BLOCK = 128


def thirds(value):
    high = value.astype(jnp.bfloat16)
    rest = value - high.astype(jnp.float32)
    middle = rest.astype(jnp.bfloat16)
    return high, middle, (rest - middle.astype(jnp.float32)).astype(jnp.bfloat16)


def exact(first, second, axis):
    high, middle, low = thirds(first)
    other_high, other_middle, other_low = thirds(second)
    left = jnp.concatenate([high, high, middle, middle, high, low], axis=1)
    right = jnp.concatenate([other_high, other_middle, other_high, other_middle, other_low, other_high], axis=axis)
    return lax.dot_general(left, right, (((1,), (axis,)), ((), ())), preferred_element_type=jnp.float32)


def exact_nn(first, second):
    return exact(first, second, 0)


def exact_nt(first, second):
    return exact(first, second, 1)


def eliminate_many(blocks):
    sub = lax.broadcasted_iota(jnp.int32, (8, BLOCK), 0)
    lane = lax.broadcasted_iota(jnp.int32, (8, BLOCK), 1)
    rows = [[block[8 * c : 8 * c + 8, :] for c in range(HALF // 8)] for block in blocks]
    for j in range(0, HALF, 4):
        home, top = j // 8, j % 8
        for chunk in rows:
            r0, r1, r2, r3 = [chunk[home][top + k : top + k + 1, :] for k in range(4)]

            def entry(row, k, j=j):
                return jnp.broadcast_to(row[:, j + k : j + k + 1], (1, BLOCK))

            p00, p01, p02, p03 = [entry(r0, k) for k in range(4)]
            p11, p12, p13 = [entry(r1, k) for k in range(1, 4)]
            p22, p23, p33 = entry(r2, 2), entry(r2, 3), entry(r3, 3)
            scale = 1.0 / (p00 * p11 - p01 * p01)
            m20, m21 = (p02 * p11 - p12 * p01) * scale, (p12 * p00 - p02 * p01) * scale
            m30, m31 = (p03 * p11 - p13 * p01) * scale, (p13 * p00 - p03 * p01) * scale
            q2 = r2 - m20 * r0 - m21 * r1
            q3 = r3 - m30 * r0 - m31 * r1
            s22 = p22 - m20 * p02 - m21 * p12
            s23 = p23 - m20 * p03 - m21 * p13
            s33 = p33 - m30 * p03 - m31 * p13
            second = 1.0 / (s22 * s33 - s23 * s23)
            t2 = (s33 * q2 - s23 * q3) * second
            t3 = (s22 * q3 - s23 * q2) * second
            t0 = (p11 * r0 - p01 * r1) * scale - m20 * t2 - m30 * t3
            t1 = (p00 * r1 - p01 * r0) * scale - m21 * t2 - m31 * t3
            final = [r0, r1 - (p01 / p00) * r0, q2, q3 - (s23 / s22) * q2]
            for c in range(home, HALF // 8):
                c0, c1, c2, c3 = [jnp.broadcast_to(chunk[c][:, j + k : j + k + 1], (8, BLOCK)) for k in range(4)]
                update = chunk[c] - ((c0 * t0 + c1 * t1) + (c2 * t2 + c3 * t3))
                if c == home:
                    update = jnp.where(sub > top + 3, update, chunk[c])
                    for k in range(1, 4):
                        update = jnp.where(sub == top + k, jnp.broadcast_to(final[k], (8, BLOCK)), update)
                chunk[c] = update
    results = []
    for chunk in rows:
        scaled_chunks = []
        for c in range(HALF // 8):
            pivot = jnp.sum(jnp.where(lane == sub + 8 * c, chunk[c], 0.0), axis=1, keepdims=True)
            scaled_chunks.append(jnp.where(lane >= HALF, chunk[c] * lax.rsqrt(pivot), 0.0))
        results.append(jnp.concatenate(scaled_chunks, axis=0))
    return results


def invert_blocks(blocks):
    lane = lax.broadcasted_iota(jnp.int32, (HALF, BLOCK), 1)
    row = lax.broadcasted_iota(jnp.int32, (HALF, BLOCK), 0)
    unit = jnp.where(lane == row + HALF, 1.0, 0.0)
    empty = jnp.zeros((HALF, BLOCK), jnp.float32)

    def tall(top):
        return jnp.concatenate([top, empty], axis=0)

    first = eliminate_many([jnp.where(lane < HALF, block[:HALF], unit) for block in blocks])
    upper = [pltpu.roll(one, HALF, 1) for one in first]
    lower = [block[HALF:] for block in blocks]
    coupling = [exact_nt(low, tall(up)) for low, up in zip(lower, upper)]
    schur = [pltpu.roll(low, HALF, 1) - exact_nt(mid, tall(mid)) for low, mid in zip(lower, coupling)]
    second = eliminate_many([jnp.where(lane < HALF, one, unit) for one in schur])
    result = []
    for up, mid, right in zip(upper, coupling, second):
        carried = exact_nn(mid, tall(up))
        left = exact_nn(pltpu.roll(right, HALF, 1), tall(carried))
        result.append(jnp.concatenate([up, right - left], axis=0))
    return result


def split(value):
    high = value.astype(jnp.bfloat16)
    return high, (value - high.astype(jnp.float32)).astype(jnp.bfloat16)


def product(high, low, other_high, other_low, contract=((1,), (0,))):
    def one(first, second):
        return lax.dot_general(first, second, (contract, ((), ())), preferred_element_type=jnp.float32)

    return one(high, other_high) + (one(high, other_low) + one(low, other_high))


def ring_chip(position, chips):
    return 2 * position + lax.div(position, chips // 2) * (2 * chips - 1 - 4 * position)


def front_kernel(
    sizes, left_ref, right_ref, slab_ref, sketch_ref, choice_ref,
    rotated_ref, basis_ref, energy_ref,
    held, other, left_full, right_full, sketch_full, left_high, left_low, weight_high, weight_low,
    part_high, part_low, image_high, image_low, second, term, term_out, term_in, outgoing, incoming,
    mail_out, mail_in, tile_out, tile_in, sums, choice_there, pivot_out, pivot_in, mid_high, mid_low,
    local_sem, choice_sem, ring_send, ring_recv, pair_send, pair_recv, cross_send, cross_recv, term_send, term_recv,
    sum_send, sum_recv, full_send, full_recv, mail_send, mail_recv, tile_send, tile_recv,
    again_send, again_recv, both_send, both_recv, far_send, far_recv, near_send, near_recv, strip_send, strip_recv, pivot_send,
    pivot_recv,
):
    chips, sectors, reach, height, order, keep, pieces = sizes
    op = lax.axis_index("op")
    sec = lax.axis_index("sec")
    core = lax.rem(op, 2)
    chip = lax.div(op, 2)
    lower = lax.div(chip, 2)
    position = lower + lax.rem(chip, 2) * (chips - 1 - 2 * lower)
    way = 1 - 2 * core

    def chip_at(steps, turn):
        return ring_chip(lax.rem(position + chips + turn * steps, chips), chips)

    ahead = {"op": 2 * chip_at(1, way) + core, "sec": sec}
    behind = {"op": 2 * chip_at(1, -way) + core, "sec": sec}
    sibling = {"op": 2 * chip + 1 - core, "sec": sec}

    def sector(distance):
        return {"op": op, "sec": lax.rem(sec + distance, sectors)}

    def remote(source, target, send, recv, device):
        return pltpu.make_async_remote_copy(
            src_ref=source, dst_ref=target, send_sem=send, recv_sem=recv, device_id=device, device_id_type=pl.DeviceIdType.MESH
        )

    started = []

    def start(copy):
        copy.start()
        started.append(copy)

    pairs = [(m, chips - m) for m in range(1, chips // 2)] + [(chips // 2, 0)]
    orders = pairs[::-1]
    blocks = [m for pair in orders for m in pair]
    copies = [
        pltpu.make_async_copy(slab_ref, held.at[0, pl.ds(0, height)], local_sem.at[0]),
        pltpu.make_async_copy(sketch_ref, sketch_full, local_sem.at[1]),
        pltpu.make_async_copy(right_ref, right_full, local_sem.at[2]),
    ]
    for copy in copies:
        copy.start()
    for place, m in enumerate(blocks):
        base = chip_at(m, -way) * 2 * height
        for side in (0, 1):
            begin = pl.multiple_of(base + (core if side == 0 else 1 - core) * height, height)
            pltpu.make_async_copy(
                left_ref.at[pl.ds(begin, height)], left_full.at[pl.ds((2 * place + side) * height, height)], local_sem.at[3]
            ).start()

    barrier = pltpu.get_barrier_semaphore()
    greeted = [ahead, behind, sibling] + [sector(d) for d in range(1, sectors)]
    for device in greeted:
        pl.semaphore_signal(barrier, inc=1, device_id=device, device_id_type=pl.DeviceIdType.MESH)
    pl.semaphore_wait(barrier, len(greeted))

    part = height // pieces

    def onward(view, m, send, recv):
        source, device = (m - 1, ahead) if m <= chips // 2 else ((m + 1) % chips, behind)
        return remote(view(source), view(m), send, recv, device)

    def after(m):
        if m == 0:
            return [1, chips - 1]
        if m < chips // 2:
            return [m + 1]
        return [m - 1] if m > chips // 2 + 1 else []

    def ring_copy(m, p):
        return onward(lambda i: held.at[0, pl.ds(i * height + p * part, part)], m, ring_send.at[m - 1, p], ring_recv.at[m - 1, p])

    def pair_copy(m, p):
        rows = pl.ds(m * height + p * part, part)
        return remote(held.at[0, rows], held.at[1, rows], pair_send.at[m, p], pair_recv.at[m, p], sibling)

    def cross_copy(d, j):
        return remote(
            held.at[0, pl.ds(j * height, height)], other.at[d - 1, pl.ds(j * height, height)], cross_send.at[d - 1, j], cross_recv.at[d - 1, j], sector(sectors - d)
        )

    crossing = [0] + [m for pair in pairs[:-1] for m in pair] + [chips // 2]

    def cross_start():
        if crossing:
            m = crossing.pop(0)
            for d in range(1, reach):
                start(cross_copy(d, m))

    copies[0].wait()
    for p in range(pieces):
        for m in after(0):
            start(ring_copy(m, p))
        start(pair_copy(0, p))
    choice_copy = remote(choice_ref, choice_there, choice_sem.at[0], choice_sem.at[1], sibling)
    start(choice_copy)
    cross_start()

    batch = 4 * height
    tile = min(512, keep)
    urgent, later = [], []

    def run(budget):
        while budget > 0 and (urgent or later):
            cost, work = (urgent or later).pop(0)
            work()
            budget -= cost

    def split_rows(source, high, low, first, count, columns):
        step = 32

        def one(i, carry):
            rows = pl.ds(pl.multiple_of(first + i * step, step), step)
            high[rows, columns], low[rows, columns] = split(source[rows, :])
            return carry

        lax.fori_loop(0, count // step, one, 0)

    def sketch_work():
        copies[1].wait()
        split_rows(sketch_full, weight_high, weight_low, 0, order, pl.ds(order + keep, keep))

    def right_work(i):
        if i == 0:
            copies[2].wait()
        split_rows(right_full, weight_high, weight_low, i * batch, batch, pl.ds(0, order))
        rows = pl.ds(i * batch, batch)
        inner = pl.ds(0, order)
        last = pl.ds(order + keep, keep)
        high, low = split(product(weight_high[rows, inner], weight_low[rows, inner], weight_high[:, last], weight_low[:, last]))
        weight_high[rows, pl.ds(order, keep)] = high
        weight_low[rows, pl.ds(order, keep)] = low

    def left_work(i):
        if i == 0:
            pltpu.make_async_copy(left_ref, left_full, local_sem.at[3]).wait()
        split_rows(left_full, left_high, left_low, i * batch, batch, pl.ds(0, order))

    def slabs_of(b):
        for m in pairs[b]:
            yield 0, m, chip_at(m, -way) * 2 + core
            yield 1, m, chip_at(m, way) * 2 + 1 - core

    def image_columns(b, columns):
        result = product(part_high[b], part_low[b], weight_high[:, columns], weight_low[:, columns])
        high, low = split(result)
        for i, (_, _, slab) in enumerate(slabs_of(b)):
            rows = pl.ds(pl.multiple_of(slab * height, height), height)
            image_high[rows, columns] = high[i * height : (i + 1) * height]
            image_low[rows, columns] = low[i * height : (i + 1) * height]

    def split_work(b):
        for i, (side, level, _) in enumerate(slabs_of(b)):
            if side == 1:
                for p in range(pieces):
                    pair_copy(level, p).wait_recv()
            high, low = split(held[side, pl.ds(level * height, height)])
            part_high[b, pl.ds(i * height, height)] = high
            part_low[b, pl.ds(i * height, height)] = low
        for column in range(0, keep, tile):
            image_columns(b, pl.ds(order + column, tile))

    def image_work(b, column):
        image_columns(b, pl.ds(column, tile))

    def second_work(b, column):
        weights = pl.ds(order + keep + column, tile)
        second[b, :, pl.ds(column, tile)] = product(part_high[b], part_low[b], weight_high[:, weights], weight_low[:, weights])

    unit = 0.75
    urgent.append((0.9, sketch_work))
    for i in range(order // batch):
        urgent.append((1.2, functools.partial(right_work, i)))
    for i in range(order // batch):
        urgent.append((0.5, functools.partial(left_work, i)))

    for b, arrivals in enumerate(pairs):
        for p in range(pieces):
            for m in arrivals:
                if m == 0:
                    continue
                ring_copy(m, p).wait_recv()
                for further in after(m):
                    start(ring_copy(further, p))
                start(pair_copy(m, p))
                if p == pieces - 1 and m == arrivals[-1] or m == chips // 2 and p == pieces - 1:
                    cross_start()
                    urgent.append((unit + 0.5, functools.partial(split_work, b)))
                    for column in range(0, order, tile):
                        later.append((unit, functools.partial(image_work, b, column)))
                    for column in range(0, keep, tile):
                        later.append((unit, functools.partial(second_work, b, column)))
                if m != chips // 2 or p < pieces - 1:
                    run(2.8 / pieces)
    while urgent:
        urgent.pop(0)[1]()

    choice_copy.wait_recv()

    def chosen(d, mine, there, shape):
        own = jnp.broadcast_to(choice_ref[0:1, 0:1], shape) == float(d)
        far = jnp.broadcast_to(choice_there[0:1, 0:1], shape) == float(d)
        return jnp.where(own, mine, 0.0) + jnp.where(far, there, 0.0)

    def half(m):
        return pl.ds(m * height, height)

    def term_copy(m):
        return remote(term_out.at[half(m)], term_in.at[half(m)], term_send.at[m], term_recv.at[m], sibling)

    def full_copy(m):
        return remote(left_full.at[pl.ds((chips + m) * height, height)], right_full.at[half(m)], full_send.at[m], full_recv.at[m], sibling)

    def halves(i, result):
        for k, m in enumerate(orders[i]):
            own = result[2 * k * height : (2 * k + 1) * height]
            yield m, own, (chips - m) % chips, result[(2 * k + 1) * height : (2 * k + 2) * height]

    def rows_of(i):
        return pl.ds(i * batch, batch)

    def term_work(i):
        for column in range(0, keep, tile):
            inner = pl.ds(order + column, tile)
            result = product(left_high[rows_of(i)], left_low[rows_of(i)], image_high[:, inner], image_low[:, inner])
            for m, own, there, far in halves(i, result):
                term[half(m), pl.ds(column, tile)] = own
                term_out[half(there), pl.ds(column, tile)] = far
        for m in orders[i]:
            term_copy((chips - m) % chips).start()

    def full_work(i, column):
        inner = pl.ds(column, tile)
        result = product(left_high[rows_of(i)], left_low[rows_of(i)], image_high[:, inner], image_low[:, inner])
        for m, own, there, far in halves(i, result):
            left_full[pl.ds(m * height, height), inner] = own
            left_full[pl.ds((chips + there) * height, height), inner] = far
        if column + tile == order:
            for m in orders[i]:
                full_copy((chips - m) % chips).start()

    done_terms = []
    for i in range(len(pairs)):
        urgent.append((unit + 0.1, lambda i=i: (term_work(i), done_terms.extend(orders[i]))))
    for i in range(len(pairs)):
        for column in range(0, order, tile):
            later.append((unit, functools.partial(full_work, i, column)))

    def sum_copy(m, d):
        device = ahead if m >= chips // 2 else behind
        return remote(outgoing.at[m - 1, d], incoming.at[m - 1, d], sum_send.at[m - 1, d], sum_recv.at[m - 1, d], device)

    shape = (height, keep)
    for r in range(chips // 2):
        steps = [(chips // 2 + r, chips // 2 + r - 1), (chips // 2 - 1 - r, chips // 2 - r)]
        for m, before in steps:
            if m == 0:
                continue
            while m not in done_terms:
                urgent.pop(0)[1]()
            term_copy(m).wait_recv()
            for d in range(reach):
                value = chosen(d, term[half(m)], term_in[half(m)], shape)
                if r > 0:
                    sum_copy(before, d).wait_recv()
                    value = value + incoming[before - 1, d]
                outgoing[m - 1, d] = value
                start(sum_copy(m, d))
                run(2.8 / reach)
        cross_start()
    while crossing:
        cross_start()
    while urgent or later:
        (urgent or later).pop(0)[1]()

    def mail_copy(d):
        return remote(mail_out.at[d - 1], mail_in.at[d - 1], mail_send.at[d - 1], mail_recv.at[d - 1], sector(d))

    def tile_copy(d):
        return remote(tile_out, tile_in.at[d - 1], tile_send.at[d - 1], tile_recv.at[d - 1], sector(d))

    term_copy(0).wait_recv()
    for d in reversed(range(reach)):
        value = chosen(d, term[half(0)], term_in[half(0)], shape)
        for before in (chips - 1, 1):
            sum_copy(before, d).wait_recv()
            value = value + incoming[before - 1, d]
        if d > 0:
            mail_out[d - 1] = value
            start(mail_copy(d))
        else:
            sums[0, 0, pl.ds(0, height)] = value

    small = (8, order)
    total = jnp.zeros(small, jnp.float32)
    for m in range(chips):
        full_copy(m).wait_recv()
        for d in range(1, reach):
            cross_copy(d, m).wait_recv()

        def add(i, carry, m=m):
            rows = pl.ds(pl.multiple_of(m * height + i * 8, 8), 8)
            for d in range(reach):
                state = held[0, rows] if d == 0 else other[d - 1, rows]
                carry = carry + state * chosen(d, left_full[rows], right_full[rows], small)
            return carry

        total = lax.fori_loop(0, height // 8, add, total)
    own = held[0, pl.ds(0, height)]
    up = jnp.broadcast_to(jnp.sum(total, keepdims=True), (8, keep))
    down = jnp.broadcast_to(jnp.sum(own * own, keepdims=True), (8, keep))
    row = lax.broadcasted_iota(jnp.int32, (8, keep), 0)
    tile_out[...] = jnp.where(row == 0, up, down)
    for m in range(chips):
        full_copy(m).wait_send()
    for copy in started[: len(started) - (reach - 1)]:
        copy.wait_send()
    del started[: len(started) - (reach - 1)]
    for d in range(1, sectors):
        start(tile_copy(d))
    for d in range(1, reach):
        mail_copy(d).wait_recv()
        sums[0, 0, pl.ds(0, height)] += mail_in[d - 1]
    both = tile_out[...]
    for d in range(1, sectors):
        tile_copy(d).wait_recv()
        both = both + tile_in[d - 1]
    sums[0, 0, pl.ds(height, 8)] = both

    spans = [pl.ds(p * part, part if p < pieces - 1 else part + 8) for p in range(pieces)]

    def again_copy(m, p):
        return onward(lambda i: sums.at[0, i, spans[p]], m, again_send.at[m - 1, p], again_recv.at[m - 1, p])

    def both_copy(m, p):
        return remote(sums.at[0, m, spans[p]], sums.at[1, m, spans[p]], both_send.at[m, p], both_recv.at[m, p], sibling)

    def row_there(side, m):
        return (2 * blocks.index(m) if side == 0 else 2 * blocks.index((chips - m) % chips) + 1) * height

    def rows_there(d, side, m):
        buffer = (left_full, right_full)[(d - 1) // 2]
        return buffer.at[pl.ds(row_there(side, m), height), pl.ds((d - 1) % 2 * keep, keep)]

    def far_copy(d, m):
        source = sums.at[0, m, pl.ds(0, height)]
        return remote(source, rows_there(d, 0, m), far_send.at[d - 1, m], far_recv.at[d - 1, m], sector(sectors - d))

    def near_copy(d, m):
        return remote(rows_there(d, 0, m), rows_there(d, 1, m), near_send.at[d - 1, m], near_recv.at[d - 1, m], sibling)

    def second_there(d, m):
        place = (d - 1) * chips + m
        return incoming.at[place // reach, place % reach]

    def other_work(d, first):
        rows = pl.ds(first * height, batch)
        high, low = split(other[d - 1, rows])
        part_high[0], part_low[0] = high, low
        for column in range(0, keep, tile):
            weights = pl.ds(order + keep + column, tile)
            result = product(part_high[0], part_low[0], weight_high[:, weights], weight_low[:, weights])
            for i in range(4):
                second_there(d, first + i)[:, pl.ds(column, tile)] = result[i * height : (i + 1) * height]

    for d in range(1, reach):
        for first in range(0, chips, 4):
            later.append((unit + 0.5, functools.partial(other_work, d, first)))
    for arrivals in [(0,)] + pairs:
        for p in range(pieces):
            for m in arrivals:
                if m == 0 and len(arrivals) > 1:
                    continue
                if m > 0:
                    again_copy(m, p).wait_recv()
                for further in after(m):
                    start(again_copy(further, p))
                start(both_copy(m, p))
                if p == pieces - 1:
                    for d in range(1, reach):
                        start(far_copy(d, m))
                run(0.1)
    while later:
        later.pop(0)[1]()
    for j in range(chips):
        for p in range(pieces):
            both_copy(j, p).wait_recv()

    both = jnp.zeros((8, keep), jnp.float32)
    for j in range(chips):
        for side in (0, 1):
            both = both + sums[side, j, pl.ds(height, 8)]
    energy = both[0:1] / both[1:2]
    at = {}
    energy_ref[...] = jnp.broadcast_to(energy, (8, keep))
    for b in range(chips // 2):
        for i, (side, m, slab) in enumerate(slabs_of(b)):
            rows = pl.ds(pl.multiple_of(slab * height, height), height)
            here = pl.ds(i * height, height)
            value = sums[side, m, pl.ds(0, height)] - energy * second[b, here]
            second[b, here] = value
            image_high[rows, pl.ds(0, keep)], image_low[rows, pl.ds(0, keep)] = split(value)
            at[side, m] = (b, here)
    for m in range(chips):
        term_copy(m).wait_send()

    def picked(shape, options):
        flag = jnp.broadcast_to(choice_ref[0:1, 0:1], shape)
        result = options[0]
        for d in range(1, reach):
            result = jnp.where(flag == float(d), options[d], result)
        return result

    gram, inverse, strips = term, term_out, term_in
    for b in range(chips // 2):
        one = exact_nn(second[b].T, second[b])
        gram[...] = one if b == 0 else gram[...] + one
    count = keep // BLOCK
    row = lax.broadcasted_iota(jnp.int32, (keep, keep), 0)
    column = lax.broadcasted_iota(jnp.int32, (keep, keep), 1)
    inverse[...] = jnp.where(row == column, 1.0, 0.0)
    inner = pl.ds(0, keep)

    def strip_there(d, b):
        return held.at[(d - 1) // 2, pl.ds(b * BLOCK, BLOCK), pl.ds((d - 1) % 2 * keep, (b + 1) * BLOCK)]

    def strip_copy(d, b):
        source = strips.at[pl.ds(b * BLOCK, BLOCK), pl.ds(0, (b + 1) * BLOCK)]
        return remote(source, strip_there(d, b), strip_send.at[d - 1, b], strip_recv.at[d - 1, b], sector(sectors - d))

    def pivot_copy(d, b):
        here = pl.ds(b * BLOCK, BLOCK)
        return remote(pivot_out.at[here], pivot_in.at[d - 1, here], pivot_send.at[d - 1, b], pivot_recv.at[d - 1, b], sector(sectors - d))

    def target_work():
        for d in range(1, reach):
            for m in range(chips):
                near_copy(d, m).wait_recv()
        step = max(1, BLOCK // (2 * height))
        for first in range(0, chips, step):
            values = []
            for m in blocks[first : first + step]:
                for side, mine in ((0, m), (1, (chips - m) % chips)):
                    place, spot = at[side, mine]
                    options = [second[place, spot]] + [rows_there(d, side, mine)[...] for d in range(1, reach)]
                    values.append(picked((height, keep), options))
            high, low = split(jnp.concatenate(values, axis=0).T)
            place = pl.ds(first * 2 * height, step * 2 * height)
            for i in range(keep // batch):
                part_high[i, :, place] = high[i * batch : (i + 1) * batch]
                part_low[i, :, place] = low[i * batch : (i + 1) * batch]
        after_left = pl.ds(2 * keep, keep)
        for i in range(keep // batch):
            result = product(part_high[i], part_low[i], image_high[:, after_left], image_low[:, after_left])
            mid_high[rows_of(i)], mid_low[rows_of(i)] = split(result)

    for b in range(count):
        here = pl.ds(b * BLOCK, BLOCK)
        upto = pl.ds(0, (b + 1) * BLOCK)
        below = pl.ds((b + 1) * BLOCK, keep - (b + 1) * BLOCK)
        strips[here, upto] = inverse[here, upto]
        for d in range(1, reach):
            start(strip_copy(d, b))
        if b == count // 2:
            for d in range(1, reach):
                for m in range(chips):
                    far_copy(d, m).wait_recv()
                    rows_there(d, 0, m)[...] = rows_there(d, 0, m)[...] - energy * second_there(d, m)[...]
                    start(near_copy(d, m))
        for part in range(order // batch) if count == 1 else range(order // batch)[b :: count - 1] if b < count - 1 else ():
            applied = product(left_high[rows_of(part)], left_low[rows_of(part)], image_high[:, inner], image_low[:, inner])
            image_high[rows_of(part), pl.ds(2 * keep, keep)], image_low[rows_of(part), pl.ds(2 * keep, keep)] = split(applied)
        if b == count - 1:
            target_work()
        pivot = invert_blocks([gram[here, here]])[0]
        pivot_out[here] = pivot
        for d in range(1, reach):
            start(pivot_copy(d, b))
        strip = exact_nn(pivot, strips[here, upto])
        inverse[here, upto] = strip
        if b < count - 1:
            low = exact_nt(gram[below, here], pivot)
            gram[below, below] = gram[below, below] - exact_nt(low, low)
            inverse[below, upto] = inverse[below, upto] - exact_nn(low, strip)

    own_high, own_low = split(inverse[...])
    across = ((1,), (1,))
    for i in range(keep // batch):
        result = product(mid_high[rows_of(i)], mid_low[rows_of(i)], own_high, own_low, across)
        mid_high[rows_of(i)], mid_low[rows_of(i)] = split(result)
    slab_high, slab_low = split(second[at[0, 0]])
    basis_ref[...] = product(slab_high, slab_low, own_high, own_low, across)
    for b in range(count):
        here = pl.ds(b * BLOCK, BLOCK)
        upto = pl.ds(0, (b + 1) * BLOCK)
        for d in range(1, reach):
            strip_copy(d, b).wait_recv()
        options = [strips[here, upto]] + [strip_there(d, b)[...] for d in range(1, reach)]
        high, low = split(picked((BLOCK, (b + 1) * BLOCK), options))
        right_high, right_low = split(product(high, low, mid_high[upto, :], mid_low[upto, :]))
        for d in range(1, reach):
            pivot_copy(d, b).wait_recv()
        options = [pivot_out[here]] + [pivot_in[d - 1, here] for d in range(1, reach)]
        high, low = split(picked((BLOCK, BLOCK), options))
        rotated_ref[here, :] = product(high, low, right_high, right_low)
    for copy in started:
        copy.wait_send()


def front(left_op, right_op, slab, sketch, choice):
    height, order = slab.shape
    keep = sketch.shape[1]
    sectors = lax.axis_size("sec")
    chips = lax.axis_size("op") // 2
    reach = min(4, sectors)
    pieces = 2
    wide, half = jnp.float32, jnp.bfloat16
    columns = order + keep
    batch = 4 * height
    dma = pltpu.SemaphoreType.DMA
    scratch = [
        ((2, chips * height, order), wide), ((reach - 1, chips * height, order), wide), ((order, order), wide),
        ((order, order), wide), ((order, keep), wide), ((order, order), half), ((order, order), half),
        ((order, columns + keep), half), ((order, columns + keep), half),
        ((chips // 2, batch, order), half), ((chips // 2, batch, order), half), ((order, columns), half), ((order, columns), half),
        ((chips // 2, batch, keep), wide), ((chips * height, keep), wide), ((chips * height, keep), wide),
        ((chips * height, keep), wide), ((chips - 1, reach, height, keep), wide), ((chips - 1, reach, height, keep), wide),
        ((reach - 1, height, keep), wide), ((reach - 1, height, keep), wide), ((8, keep), wide), ((sectors - 1, 8, keep), wide),
        ((2, chips, height + 8, keep), wide), ((8, 128), wide), ((keep, BLOCK), wide), ((reach - 1, keep, BLOCK), wide), ((keep, keep), half), ((keep, keep), half),
    ]
    counts = [
        (4,), (2,), (chips - 1, pieces), (chips - 1, pieces), (chips, pieces), (chips, pieces), (reach - 1, chips),
        (reach - 1, chips), (chips,), (chips,), (chips - 1, reach), (chips - 1, reach), (chips,), (chips,), (reach - 1,),
        (reach - 1,), (sectors - 1,), (sectors - 1,), (chips - 1, pieces), (chips - 1, pieces), (chips, pieces), (chips, pieces),
        (reach - 1, chips), (reach - 1, chips), (reach - 1, chips), (reach - 1, chips), (reach - 1, keep // BLOCK),
        (reach - 1, keep // BLOCK), (reach - 1, keep // BLOCK), (reach - 1, keep // BLOCK),
    ]
    anywhere = pl.BlockSpec(memory_space=pl.ANY)
    inside = pl.BlockSpec(memory_space=pltpu.VMEM)
    sizes = (chips, sectors, reach, height, order, keep, pieces)
    return pl.pallas_call(
        functools.partial(front_kernel, sizes),
        out_shape=tuple(jax.ShapeDtypeStruct((rows, keep), wide) for rows in (keep, height, 8)),
        in_specs=[anywhere] * 4 + [inside],
        out_specs=(inside, inside, inside),
        scratch_shapes=[pltpu.VMEM(shape, kind) for shape, kind in scratch] + [dma(count) for count in counts],
        compiler_params=pltpu.CompilerParams(collective_id=0, has_side_effects=True, vmem_limit_bytes=63 * 2**20),
        cost_estimate=pl.CostEstimate(flops=24 * order**3, bytes_accessed=48 * order**2, transcendentals=0),
        name="front",
    )(left_op, right_op, slab, sketch, choice)


def finish_kernel(rotated_ref, basis_ref, quotient_ref, rotated_out, basis_out, energy_out):
    rotated_out[...] = rotated_ref[...]
    basis_out[...] = basis_ref[...]
    energy_out[0, 0] = quotient_ref[0, 0]


def finish(rotated, basis_slab, quotient):
    inside = pl.BlockSpec(memory_space=pltpu.VMEM)
    scalar = pl.BlockSpec(memory_space=pltpu.SMEM)
    shapes = (rotated.shape, basis_slab.shape, (1, 1))
    return pl.pallas_call(
        finish_kernel,
        out_shape=tuple(jax.ShapeDtypeStruct(shape, jnp.float32) for shape in shapes),
        in_specs=[inside] * 3,
        out_specs=(inside, inside, scalar),
        name="finish",
    )(rotated, basis_slab, quotient)


def body(left_ops, right_ops, amplitudes, sketch, sector_shift):
    left_op = left_ops[0, 0]
    sectors = lax.axis_size("sec")
    height = amplitudes.shape[1]
    choice = lax.rem(sector_shift[0], sectors)
    flag = jnp.full((8, 128), choice.astype(jnp.float32))
    results = front(left_op, right_ops[0, 0], amplitudes[0], sketch, flag)
    rotated, basis_slab, energy = finish(*results)
    return (rotated[None, None], basis_slab[None], energy.reshape(()))


def solution(mesh):
    in_specs = (
        P("op", "sec", None, None),
        P("op", "sec", None, None),
        P("sec", "op", None),
        P(),
        P("op"),
    )
    out_specs = (P("op", "sec", None, None), P("sec", "op", None), P())
    return jax.shard_map(body, mesh=mesh, in_specs=in_specs, out_specs=out_specs, check_vma=False)
```

```python
import functools

import jax
import jax.numpy as jnp
from jax import lax
from jax.experimental import pallas as pl
from jax.experimental.pallas import tpu as pltpu
from jax.sharding import PartitionSpec as P

HALF = 64
BLOCK = 128


def thirds(value):
    high = value.astype(jnp.bfloat16)
    rest = value - high.astype(jnp.float32)
    middle = rest.astype(jnp.bfloat16)
    return high, middle, (rest - middle.astype(jnp.float32)).astype(jnp.bfloat16)


def laid(value, places, axis):
    parts = thirds(value)
    return jnp.concatenate([parts[place] for place in places], axis=axis)


FIRST = (0, 0, 1, 1, 0, 2)
SECOND = (0, 1, 0, 1, 2, 0)


def summed(left, right, axis):
    return lax.dot_general(left, right, (((1,), (axis,)), ((), ())), preferred_element_type=jnp.float32)


def exact(first, second, axis):
    return summed(laid(first, FIRST, 1), laid(second, SECOND, axis), axis)


def exact_nn(first, second):
    return exact(first, second, 0)


def exact_nt(first, second):
    return exact(first, second, 1)


def eliminate_many(blocks):
    sub = lax.broadcasted_iota(jnp.int32, (8, BLOCK), 0)
    lane = lax.broadcasted_iota(jnp.int32, (8, BLOCK), 1)
    rows = [[block[8 * c : 8 * c + 8, :] for c in range(HALF // 8)] for block in blocks]
    for j in range(0, HALF, 4):
        home, top = j // 8, j % 8
        for chunk in rows:
            r0, r1, r2, r3 = [chunk[home][top + k : top + k + 1, :] for k in range(4)]

            def entry(row, k, j=j):
                return jnp.broadcast_to(row[:, j + k : j + k + 1], (1, BLOCK))

            p00, p01, p02, p03 = [entry(r0, k) for k in range(4)]
            p11, p12, p13 = [entry(r1, k) for k in range(1, 4)]
            p22, p23, p33 = entry(r2, 2), entry(r2, 3), entry(r3, 3)
            scale = 1.0 / (p00 * p11 - p01 * p01)
            m20, m21 = (p02 * p11 - p12 * p01) * scale, (p12 * p00 - p02 * p01) * scale
            m30, m31 = (p03 * p11 - p13 * p01) * scale, (p13 * p00 - p03 * p01) * scale
            q2 = r2 - m20 * r0 - m21 * r1
            q3 = r3 - m30 * r0 - m31 * r1
            s22 = p22 - m20 * p02 - m21 * p12
            s23 = p23 - m20 * p03 - m21 * p13
            s33 = p33 - m30 * p03 - m31 * p13
            second = 1.0 / (s22 * s33 - s23 * s23)
            t2 = (s33 * q2 - s23 * q3) * second
            t3 = (s22 * q3 - s23 * q2) * second
            t0 = (p11 * r0 - p01 * r1) * scale - m20 * t2 - m30 * t3
            t1 = (p00 * r1 - p01 * r0) * scale - m21 * t2 - m31 * t3
            final = [r0, r1 - (p01 / p00) * r0, q2, q3 - (s23 / s22) * q2]
            for c in range(home, HALF // 8):
                c0, c1, c2, c3 = [jnp.broadcast_to(chunk[c][:, j + k : j + k + 1], (8, BLOCK)) for k in range(4)]
                update = chunk[c] - ((c0 * t0 + c1 * t1) + (c2 * t2 + c3 * t3))
                if c == home:
                    update = jnp.where(sub > top + 3, update, chunk[c])
                    for k in range(1, 4):
                        update = jnp.where(sub == top + k, jnp.broadcast_to(final[k], (8, BLOCK)), update)
                chunk[c] = update
    results = []
    for chunk in rows:
        scaled_chunks = []
        for c in range(HALF // 8):
            pivot = jnp.sum(jnp.where(lane == sub + 8 * c, chunk[c], 0.0), axis=1, keepdims=True)
            scaled_chunks.append(jnp.where(lane >= HALF, chunk[c] * lax.rsqrt(pivot), 0.0))
        results.append(jnp.concatenate(scaled_chunks, axis=0))
    return results


def invert_blocks(blocks):
    lane = lax.broadcasted_iota(jnp.int32, (HALF, BLOCK), 1)
    row = lax.broadcasted_iota(jnp.int32, (HALF, BLOCK), 0)
    unit = jnp.where(lane == row + HALF, 1.0, 0.0)
    empty = jnp.zeros((HALF, BLOCK), jnp.float32)

    def tall(top):
        return jnp.concatenate([top, empty], axis=0)

    first = eliminate_many([jnp.where(lane < HALF, block[:HALF], unit) for block in blocks])
    upper = [pltpu.roll(one, HALF, 1) for one in first]
    lower = [block[HALF:] for block in blocks]
    coupling = [exact_nt(low, tall(up)) for low, up in zip(lower, upper)]
    schur = [pltpu.roll(low, HALF, 1) - exact_nt(mid, tall(mid)) for low, mid in zip(lower, coupling)]
    second = eliminate_many([jnp.where(lane < HALF, one, unit) for one in schur])
    result = []
    for up, mid, right in zip(upper, coupling, second):
        carried = exact_nn(mid, tall(up))
        left = exact_nn(pltpu.roll(right, HALF, 1), tall(carried))
        result.append(jnp.concatenate([up, right - left], axis=0))
    return result


def split(value):
    high = value.astype(jnp.bfloat16)
    return high, (value - high.astype(jnp.float32)).astype(jnp.bfloat16)


def product(high, low, other_high, other_low, contract=((1,), (0,))):
    def one(first, second):
        return lax.dot_general(first, second, (contract, ((), ())), preferred_element_type=jnp.float32)

    return one(high, other_high) + (one(high, other_low) + one(low, other_high))


def ring_chip(position, chips):
    return 2 * position + lax.div(position, chips // 2) * (2 * chips - 1 - 4 * position)


def front_kernel(
    sizes, left_ref, right_ref, slab_ref, sketch_ref, choice_ref,
    rotated_ref, basis_ref, energy_ref,
    held, other, left_full, right_full, sketch_full, left_high, left_low, weight_high, weight_low,
    part_high, part_low, image_high, image_low, second, term, term_out, term_in, outgoing, incoming,
    mail_out, mail_in, tile_out, tile_in, sums, choice_there, pivot_out, pivot_in, mid_high, mid_low,
    local_sem, choice_sem, ring_send, ring_recv, pair_send, pair_recv, cross_send, cross_recv, term_send, term_recv,
    sum_send, sum_recv, full_send, full_recv, mail_send, mail_recv, tile_send, tile_recv,
    again_send, again_recv, both_send, both_recv, far_send, far_recv, near_send, near_recv, strip_send, strip_recv, pivot_send,
    pivot_recv,
):
    chips, sectors, reach, height, order, keep, pieces = sizes
    op = lax.axis_index("op")
    sec = lax.axis_index("sec")
    core = lax.rem(op, 2)
    chip = lax.div(op, 2)
    lower = lax.div(chip, 2)
    position = lower + lax.rem(chip, 2) * (chips - 1 - 2 * lower)
    way = 1 - 2 * core

    def chip_at(steps, turn):
        return ring_chip(lax.rem(position + chips + turn * steps, chips), chips)

    ahead = {"op": 2 * chip_at(1, way) + core, "sec": sec}
    behind = {"op": 2 * chip_at(1, -way) + core, "sec": sec}
    sibling = {"op": 2 * chip + 1 - core, "sec": sec}

    def sector(distance):
        return {"op": op, "sec": lax.rem(sec + distance, sectors)}

    def remote(source, target, send, recv, device):
        return pltpu.make_async_remote_copy(
            src_ref=source, dst_ref=target, send_sem=send, recv_sem=recv, device_id=device, device_id_type=pl.DeviceIdType.MESH
        )

    started = []

    def start(copy):
        copy.start()
        started.append(copy)

    pairs = [(m, chips - m) for m in range(1, chips // 2)] + [(chips // 2, 0)]
    orders = pairs[::-1]
    blocks = [m for pair in orders for m in pair]
    copies = [
        pltpu.make_async_copy(slab_ref, held.at[0, pl.ds(0, height)], local_sem.at[0]),
        pltpu.make_async_copy(sketch_ref, sketch_full, local_sem.at[1]),
        pltpu.make_async_copy(right_ref, right_full, local_sem.at[2]),
    ]
    for copy in copies:
        copy.start()
    for place, m in enumerate(blocks):
        base = chip_at(m, -way) * 2 * height
        for side in (0, 1):
            begin = pl.multiple_of(base + (core if side == 0 else 1 - core) * height, height)
            pltpu.make_async_copy(
                left_ref.at[pl.ds(begin, height)], left_full.at[pl.ds((2 * place + side) * height, height)], local_sem.at[3]
            ).start()

    barrier = pltpu.get_barrier_semaphore()
    greeted = [ahead, behind, sibling] + [sector(d) for d in range(1, sectors)]
    for device in greeted:
        pl.semaphore_signal(barrier, inc=1, device_id=device, device_id_type=pl.DeviceIdType.MESH)
    pl.semaphore_wait(barrier, len(greeted))

    part = height // pieces

    def onward(view, m, send, recv):
        source, device = (m - 1, ahead) if m <= chips // 2 else ((m + 1) % chips, behind)
        return remote(view(source), view(m), send, recv, device)

    def after(m):
        if m == 0:
            return [1, chips - 1]
        if m < chips // 2:
            return [m + 1]
        return [m - 1] if m > chips // 2 + 1 else []

    def ring_copy(m, p):
        return onward(lambda i: held.at[0, pl.ds(i * height + p * part, part)], m, ring_send.at[m - 1, p], ring_recv.at[m - 1, p])

    def pair_copy(m, p):
        rows = pl.ds(m * height + p * part, part)
        return remote(held.at[0, rows], held.at[1, rows], pair_send.at[m, p], pair_recv.at[m, p], sibling)

    def cross_copy(d, j):
        return remote(
            held.at[0, pl.ds(j * height, height)], other.at[d - 1, pl.ds(j * height, height)], cross_send.at[d - 1, j], cross_recv.at[d - 1, j], sector(sectors - d)
        )

    crossing = [0] + [m for pair in pairs[:-1] for m in pair] + [chips // 2]

    def cross_start():
        if crossing:
            m = crossing.pop(0)
            for d in range(1, reach):
                start(cross_copy(d, m))

    copies[0].wait()
    for p in range(pieces):
        for m in after(0):
            start(ring_copy(m, p))
        start(pair_copy(0, p))
    choice_copy = remote(choice_ref, choice_there, choice_sem.at[0], choice_sem.at[1], sibling)
    start(choice_copy)
    cross_start()

    batch = 4 * height
    tile = min(512, keep)
    urgent, later = [], []

    def run(budget):
        while budget > 0 and (urgent or later):
            cost, work = (urgent or later).pop(0)
            work()
            budget -= cost

    def split_rows(source, high, low, first, count, columns):
        step = 32

        def one(i, carry):
            rows = pl.ds(pl.multiple_of(first + i * step, step), step)
            high[rows, columns], low[rows, columns] = split(source[rows, :])
            return carry

        lax.fori_loop(0, count // step, one, 0)

    def sketch_work():
        copies[1].wait()
        split_rows(sketch_full, weight_high, weight_low, 0, order, pl.ds(order + keep, keep))

    def right_work(i):
        if i == 0:
            copies[2].wait()
        split_rows(right_full, weight_high, weight_low, i * batch, batch, pl.ds(0, order))
        rows = pl.ds(i * batch, batch)
        inner = pl.ds(0, order)
        last = pl.ds(order + keep, keep)
        high, low = split(product(weight_high[rows, inner], weight_low[rows, inner], weight_high[:, last], weight_low[:, last]))
        weight_high[rows, pl.ds(order, keep)] = high
        weight_low[rows, pl.ds(order, keep)] = low

    def left_work(i):
        if i == 0:
            pltpu.make_async_copy(left_ref, left_full, local_sem.at[3]).wait()
        split_rows(left_full, left_high, left_low, i * batch, batch, pl.ds(0, order))

    def slabs_of(b):
        for m in pairs[b]:
            yield 0, m, chip_at(m, -way) * 2 + core
            yield 1, m, chip_at(m, way) * 2 + 1 - core

    def image_columns(b, columns):
        result = product(part_high[b], part_low[b], weight_high[:, columns], weight_low[:, columns])
        high, low = split(result)
        for i, (_, _, slab) in enumerate(slabs_of(b)):
            rows = pl.ds(pl.multiple_of(slab * height, height), height)
            image_high[rows, columns] = high[i * height : (i + 1) * height]
            image_low[rows, columns] = low[i * height : (i + 1) * height]

    def split_work(b):
        for i, (side, level, _) in enumerate(slabs_of(b)):
            if side == 1:
                for p in range(pieces):
                    pair_copy(level, p).wait_recv()
            high, low = split(held[side, pl.ds(level * height, height)])
            part_high[b, pl.ds(i * height, height)] = high
            part_low[b, pl.ds(i * height, height)] = low
        for column in range(0, keep, tile):
            image_columns(b, pl.ds(order + column, tile))

    def image_work(b, column):
        image_columns(b, pl.ds(column, tile))

    def second_work(b, column):
        weights = pl.ds(order + keep + column, tile)
        second[b, :, pl.ds(column, tile)] = product(part_high[b], part_low[b], weight_high[:, weights], weight_low[:, weights])

    unit = 0.75
    urgent.append((0.9, sketch_work))
    for i in range(order // batch):
        urgent.append((1.2, functools.partial(right_work, i)))
    for i in range(order // batch):
        urgent.append((0.5, functools.partial(left_work, i)))

    for b, arrivals in enumerate(pairs):
        for p in range(pieces):
            for m in arrivals:
                if m == 0:
                    continue
                ring_copy(m, p).wait_recv()
                for further in after(m):
                    start(ring_copy(further, p))
                start(pair_copy(m, p))
                if p == pieces - 1 and m == arrivals[-1] or m == chips // 2 and p == pieces - 1:
                    for _ in arrivals:
                        cross_start()
                    urgent.append((unit + 0.5, functools.partial(split_work, b)))
                    for column in range(0, order, tile):
                        later.append((unit, functools.partial(image_work, b, column)))
                    for column in range(0, keep, tile):
                        later.append((unit, functools.partial(second_work, b, column)))
                if m != chips // 2 or p < pieces - 1:
                    run(2.8 / pieces)
    while urgent:
        urgent.pop(0)[1]()

    choice_copy.wait_recv()

    def chosen(d, mine, there, shape):
        own = jnp.broadcast_to(choice_ref[0:1, 0:1], shape) == float(d)
        far = jnp.broadcast_to(choice_there[0:1, 0:1], shape) == float(d)
        return jnp.where(own, mine, 0.0) + jnp.where(far, there, 0.0)

    def half(m):
        return pl.ds(m * height, height)

    def term_copy(m):
        return remote(term_out.at[half(m)], term_in.at[half(m)], term_send.at[m], term_recv.at[m], sibling)

    def full_copy(m):
        return remote(left_full.at[pl.ds((chips + m) * height, height)], right_full.at[half(m)], full_send.at[m], full_recv.at[m], sibling)

    def halves(i, result):
        for k, m in enumerate(orders[i]):
            own = result[2 * k * height : (2 * k + 1) * height]
            yield m, own, (chips - m) % chips, result[(2 * k + 1) * height : (2 * k + 2) * height]

    def rows_of(i):
        return pl.ds(i * batch, batch)

    def term_work(i):
        for column in range(0, keep, tile):
            inner = pl.ds(order + column, tile)
            result = product(left_high[rows_of(i)], left_low[rows_of(i)], image_high[:, inner], image_low[:, inner])
            for m, own, there, far in halves(i, result):
                term[half(m), pl.ds(column, tile)] = own
                term_out[half(there), pl.ds(column, tile)] = far
        for m in orders[i]:
            term_copy((chips - m) % chips).start()

    def full_work(i, column):
        inner = pl.ds(column, tile)
        result = product(left_high[rows_of(i)], left_low[rows_of(i)], image_high[:, inner], image_low[:, inner])
        for m, own, there, far in halves(i, result):
            left_full[pl.ds(m * height, height), inner] = own
            left_full[pl.ds((chips + there) * height, height), inner] = far
        if column + tile == order:
            for m in orders[i]:
                full_copy((chips - m) % chips).start()

    done_terms = []
    for i in range(len(pairs)):
        urgent.append((unit + 0.1, lambda i=i: (term_work(i), done_terms.extend(orders[i]))))
    for i in range(len(pairs)):
        for column in range(0, order, tile):
            later.append((unit, functools.partial(full_work, i, column)))

    def sum_copy(m, d):
        device = ahead if m >= chips // 2 else behind
        return remote(outgoing.at[m - 1, d], incoming.at[m - 1, d], sum_send.at[m - 1, d], sum_recv.at[m - 1, d], device)

    shape = (height, keep)
    summing = []
    for r in range(chips // 2):
        steps = [(chips // 2 + r, chips // 2 + r - 1), (chips // 2 - 1 - r, chips // 2 - r)]
        for m, before in steps:
            if m == 0:
                continue
            while m not in done_terms:
                urgent.pop(0)[1]()
            term_copy(m).wait_recv()
            for d in range(reach):
                value = chosen(d, term[half(m)], term_in[half(m)], shape)
                if r > 0:
                    sum_copy(before, d).wait_recv()
                    value = value + incoming[before - 1, d]
                outgoing[m - 1, d] = value
                sum_copy(m, d).start()
                summing.append(sum_copy(m, d))
                run(2.8 / reach)
        cross_start()
    while crossing:
        cross_start()
    while urgent or later:
        (urgent or later).pop(0)[1]()

    def mail_copy(d):
        return remote(mail_out.at[d - 1], mail_in.at[d - 1], mail_send.at[d - 1], mail_recv.at[d - 1], sector(d))

    def tile_copy(d):
        return remote(tile_out, tile_in.at[d - 1], tile_send.at[d - 1], tile_recv.at[d - 1], sector(d))

    small = (8, order)
    total = jnp.zeros(small, jnp.float32)
    for m in range(chips):
        full_copy(m).wait_recv()
        for d in range(1, reach):
            cross_copy(d, m).wait_recv()

        def add(i, carry, m=m):
            rows = pl.ds(pl.multiple_of(m * height + i * 8, 8), 8)
            for d in range(reach):
                state = held[0, rows] if d == 0 else other[d - 1, rows]
                carry = carry + state * chosen(d, left_full[rows], right_full[rows], small)
            return carry

        total = lax.fori_loop(0, height // 8, add, total)
    own = held[0, pl.ds(0, height)]
    up = jnp.broadcast_to(jnp.sum(total, keepdims=True), (8, keep))
    down = jnp.broadcast_to(jnp.sum(own * own, keepdims=True), (8, keep))
    row = lax.broadcasted_iota(jnp.int32, (8, keep), 0)
    tile_out[...] = jnp.where(row == 0, up, down)
    for m in range(chips):
        full_copy(m).wait_send()
    for copy in started:
        copy.wait_send()
    started[:] = summing
    for d in range(1, sectors):
        start(tile_copy(d))
    term_copy(0).wait_recv()
    for d in reversed(range(reach)):
        value = chosen(d, term[half(0)], term_in[half(0)], shape)
        for before in (chips - 1, 1):
            sum_copy(before, d).wait_recv()
            value = value + incoming[before - 1, d]
        if d > 0:
            mail_out[d - 1] = value
            start(mail_copy(d))
        else:
            sums[0, 0, pl.ds(0, height)] = value

    for d in range(1, reach):
        mail_copy(d).wait_recv()
        sums[0, 0, pl.ds(0, height)] += mail_in[d - 1]
    both = tile_out[...]
    for d in range(1, sectors):
        tile_copy(d).wait_recv()
        both = both + tile_in[d - 1]
    sums[0, 0, pl.ds(height, 8)] = both

    spans = [pl.ds(p * part, part if p < pieces - 1 else part + 8) for p in range(pieces)]

    def again_copy(m, p):
        return onward(lambda i: sums.at[0, i, spans[p]], m, again_send.at[m - 1, p], again_recv.at[m - 1, p])

    def both_copy(m, p):
        return remote(sums.at[0, m, spans[p]], sums.at[1, m, spans[p]], both_send.at[m, p], both_recv.at[m, p], sibling)

    def row_there(side, m):
        return (2 * blocks.index(m) if side == 0 else 2 * blocks.index((chips - m) % chips) + 1) * height

    def rows_there(d, side, m):
        buffer = (left_full, right_full)[(d - 1) // 2]
        return buffer.at[pl.ds(row_there(side, m), height), pl.ds((d - 1) % 2 * keep, keep)]

    def far_copy(d, m):
        source = sums.at[0, m, pl.ds(0, height)]
        return remote(source, rows_there(d, 0, m), far_send.at[d - 1, m], far_recv.at[d - 1, m], sector(sectors - d))

    def near_copy(d, m):
        return remote(rows_there(d, 0, m), rows_there(d, 1, m), near_send.at[d - 1, m], near_recv.at[d - 1, m], sibling)

    def second_there(d, m):
        place = (d - 1) * chips + m
        return incoming.at[place // reach, place % reach]

    def other_work(d, first):
        rows = pl.ds(first * height, batch)
        high, low = split(other[d - 1, rows])
        part_high[0], part_low[0] = high, low
        for column in range(0, keep, tile):
            weights = pl.ds(order + keep + column, tile)
            result = product(part_high[0], part_low[0], weight_high[:, weights], weight_low[:, weights])
            for i in range(4):
                second_there(d, first + i)[:, pl.ds(column, tile)] = result[i * height : (i + 1) * height]

    for d in range(1, reach):
        for first in range(0, chips, 4):
            later.append((unit + 0.5, functools.partial(other_work, d, first)))
    for arrivals in [(0,)] + pairs:
        for p in range(pieces):
            for m in arrivals:
                if m == 0 and len(arrivals) > 1:
                    continue
                if m > 0:
                    again_copy(m, p).wait_recv()
                for further in after(m):
                    start(again_copy(further, p))
                start(both_copy(m, p))
                if p == pieces - 1:
                    for d in range(1, reach):
                        start(far_copy(d, m))
                run(0.1)
    while later:
        later.pop(0)[1]()
    for j in range(chips):
        for p in range(pieces):
            both_copy(j, p).wait_recv()

    both = jnp.zeros((8, keep), jnp.float32)
    for j in range(chips):
        for side in (0, 1):
            both = both + sums[side, j, pl.ds(height, 8)]
    energy = both[0:1] / both[1:2]
    at = {}
    energy_ref[...] = jnp.broadcast_to(energy, (8, keep))
    for b in range(chips // 2):
        for i, (side, m, slab) in enumerate(slabs_of(b)):
            rows = pl.ds(pl.multiple_of(slab * height, height), height)
            here = pl.ds(i * height, height)
            value = sums[side, m, pl.ds(0, height)] - energy * second[b, here]
            second[b, here] = value
            image_high[rows, pl.ds(0, keep)], image_low[rows, pl.ds(0, keep)] = split(value)
            at[side, m] = (b, here)
    for m in range(chips):
        term_copy(m).wait_send()

    def picked(shape, options):
        flag = jnp.broadcast_to(choice_ref[0:1, 0:1], shape)
        result = options[0]
        for d in range(1, reach):
            result = jnp.where(flag == float(d), options[d], result)
        return result

    gram, inverse, strips = term, term_out, term_in
    middle = keep // 2 // BLOCK * BLOCK
    for b in range(chips // 2):
        left, right = laid(second[b].T, FIRST, 1), laid(second[b], SECOND, 0)
        for first, width in ((0, middle), (middle, keep - middle)):
            lower, across = pl.ds(first, keep - first), pl.ds(first, width)
            one = summed(left[first:], right[:, first : first + width], 0)
            gram[lower, across] = one if b == 0 else gram[lower, across] + one
    count = keep // BLOCK
    row = lax.broadcasted_iota(jnp.int32, (keep, keep), 0)
    column = lax.broadcasted_iota(jnp.int32, (keep, keep), 1)
    inverse[...] = jnp.where(row == column, 1.0, 0.0)
    inner = pl.ds(0, keep)

    def strip_there(d, b):
        return held.at[(d - 1) // 2, pl.ds(b * BLOCK, BLOCK), pl.ds((d - 1) % 2 * keep, (b + 1) * BLOCK)]

    def strip_copy(d, b):
        source = strips.at[pl.ds(b * BLOCK, BLOCK), pl.ds(0, (b + 1) * BLOCK)]
        return remote(source, strip_there(d, b), strip_send.at[d - 1, b], strip_recv.at[d - 1, b], sector(sectors - d))

    def pivot_copy(d, b):
        here = pl.ds(b * BLOCK, BLOCK)
        return remote(pivot_out.at[here], pivot_in.at[d - 1, here], pivot_send.at[d - 1, b], pivot_recv.at[d - 1, b], sector(sectors - d))

    def target_work():
        for d in range(1, reach):
            for m in range(chips):
                near_copy(d, m).wait_recv()
        step = max(1, BLOCK // (2 * height))
        for first in range(0, chips, step):
            values = []
            for m in blocks[first : first + step]:
                for side, mine in ((0, m), (1, (chips - m) % chips)):
                    place, spot = at[side, mine]
                    options = [second[place, spot]] + [rows_there(d, side, mine)[...] for d in range(1, reach)]
                    values.append(picked((height, keep), options))
            high, low = split(jnp.concatenate(values, axis=0).T)
            place = pl.ds(first * 2 * height, step * 2 * height)
            for i in range(keep // batch):
                part_high[i, :, place] = high[i * batch : (i + 1) * batch]
                part_low[i, :, place] = low[i * batch : (i + 1) * batch]
        after_left = pl.ds(2 * keep, keep)
        for i in range(keep // batch):
            result = product(part_high[i], part_low[i], image_high[:, after_left], image_low[:, after_left])
            mid_high[rows_of(i)], mid_low[rows_of(i)] = split(result)

    for b in range(count):
        here = pl.ds(b * BLOCK, BLOCK)
        upto = pl.ds(0, (b + 1) * BLOCK)
        below = pl.ds((b + 1) * BLOCK, keep - (b + 1) * BLOCK)
        strips[here, upto] = inverse[here, upto]
        for d in range(1, reach):
            start(strip_copy(d, b))
        if b == count // 2:
            for d in range(1, reach):
                for m in range(chips):
                    far_copy(d, m).wait_recv()
                    rows_there(d, 0, m)[...] = rows_there(d, 0, m)[...] - energy * second_there(d, m)[...]
                    start(near_copy(d, m))
        for part in range(order // batch) if count == 1 else range(order // batch)[b :: count - 1] if b < count - 1 else ():
            applied = product(left_high[rows_of(part)], left_low[rows_of(part)], image_high[:, inner], image_low[:, inner])
            image_high[rows_of(part), pl.ds(2 * keep, keep)], image_low[rows_of(part), pl.ds(2 * keep, keep)] = split(applied)
        if b == count - 1:
            target_work()
        pivot = invert_blocks([gram[here, here]])[0]
        pivot_out[here] = pivot
        for d in range(1, reach):
            start(pivot_copy(d, b))
        strip = exact_nn(pivot, strips[here, upto])
        inverse[here, upto] = strip
        if b < count - 1:
            low = exact_nt(gram[below, here], pivot)
            gram[below, below] = gram[below, below] - exact_nt(low, low)
            inverse[below, upto] = inverse[below, upto] - exact_nn(low, strip)

    own_high, own_low = split(inverse[...])
    across = ((1,), (1,))
    for i in range(keep // batch):
        result = product(mid_high[rows_of(i)], mid_low[rows_of(i)], own_high, own_low, across)
        mid_high[rows_of(i)], mid_low[rows_of(i)] = split(result)
    slab_high, slab_low = split(second[at[0, 0]])
    basis_ref[...] = product(slab_high, slab_low, own_high, own_low, across)
    for b in range(count):
        here = pl.ds(b * BLOCK, BLOCK)
        upto = pl.ds(0, (b + 1) * BLOCK)
        for d in range(1, reach):
            strip_copy(d, b).wait_recv()
        options = [strips[here, upto]] + [strip_there(d, b)[...] for d in range(1, reach)]
        high, low = split(picked((BLOCK, (b + 1) * BLOCK), options))
        right_high, right_low = split(product(high, low, mid_high[upto, :], mid_low[upto, :]))
        for d in range(1, reach):
            pivot_copy(d, b).wait_recv()
        options = [pivot_out[here]] + [pivot_in[d - 1, here] for d in range(1, reach)]
        high, low = split(picked((BLOCK, BLOCK), options))
        rotated_ref[here, :] = product(high, low, right_high, right_low)
    for copy in started:
        copy.wait_send()


def front(left_op, right_op, slab, sketch, choice):
    height, order = slab.shape
    keep = sketch.shape[1]
    sectors = lax.axis_size("sec")
    chips = lax.axis_size("op") // 2
    reach = min(4, sectors)
    pieces = 2
    wide, half = jnp.float32, jnp.bfloat16
    columns = order + keep
    batch = 4 * height
    dma = pltpu.SemaphoreType.DMA
    scratch = [
        ((2, chips * height, order), wide), ((reach - 1, chips * height, order), wide), ((order, order), wide),
        ((order, order), wide), ((order, keep), wide), ((order, order), half), ((order, order), half),
        ((order, columns + keep), half), ((order, columns + keep), half),
        ((chips // 2, batch, order), half), ((chips // 2, batch, order), half), ((order, columns), half), ((order, columns), half),
        ((chips // 2, batch, keep), wide), ((chips * height, keep), wide), ((chips * height, keep), wide),
        ((chips * height, keep), wide), ((chips - 1, reach, height, keep), wide), ((chips - 1, reach, height, keep), wide),
        ((reach - 1, height, keep), wide), ((reach - 1, height, keep), wide), ((8, keep), wide), ((sectors - 1, 8, keep), wide),
        ((2, chips, height + 8, keep), wide), ((8, 128), wide), ((keep, BLOCK), wide), ((reach - 1, keep, BLOCK), wide), ((keep, keep), half), ((keep, keep), half),
    ]
    counts = [
        (4,), (2,), (chips - 1, pieces), (chips - 1, pieces), (chips, pieces), (chips, pieces), (reach - 1, chips),
        (reach - 1, chips), (chips,), (chips,), (chips - 1, reach), (chips - 1, reach), (chips,), (chips,), (reach - 1,),
        (reach - 1,), (sectors - 1,), (sectors - 1,), (chips - 1, pieces), (chips - 1, pieces), (chips, pieces), (chips, pieces),
        (reach - 1, chips), (reach - 1, chips), (reach - 1, chips), (reach - 1, chips), (reach - 1, keep // BLOCK),
        (reach - 1, keep // BLOCK), (reach - 1, keep // BLOCK), (reach - 1, keep // BLOCK),
    ]
    anywhere = pl.BlockSpec(memory_space=pl.ANY)
    inside = pl.BlockSpec(memory_space=pltpu.VMEM)
    sizes = (chips, sectors, reach, height, order, keep, pieces)
    return pl.pallas_call(
        functools.partial(front_kernel, sizes),
        out_shape=tuple(jax.ShapeDtypeStruct((rows, keep), wide) for rows in (keep, height, 8)),
        in_specs=[anywhere] * 4 + [inside],
        out_specs=(inside, inside, inside),
        scratch_shapes=[pltpu.VMEM(shape, kind) for shape, kind in scratch] + [dma(count) for count in counts],
        compiler_params=pltpu.CompilerParams(collective_id=0, has_side_effects=True, vmem_limit_bytes=63 * 2**20),
        cost_estimate=pl.CostEstimate(flops=24 * order**3, bytes_accessed=48 * order**2, transcendentals=0),
        name="front",
    )(left_op, right_op, slab, sketch, choice)


def finish_kernel(rotated_ref, basis_ref, quotient_ref, rotated_out, basis_out, energy_out):
    rotated_out[...] = rotated_ref[...]
    basis_out[...] = basis_ref[...]
    energy_out[0, 0] = quotient_ref[0, 0]


def finish(rotated, basis_slab, quotient):
    inside = pl.BlockSpec(memory_space=pltpu.VMEM)
    scalar = pl.BlockSpec(memory_space=pltpu.SMEM)
    shapes = (rotated.shape, basis_slab.shape, (1, 1))
    return pl.pallas_call(
        finish_kernel,
        out_shape=tuple(jax.ShapeDtypeStruct(shape, jnp.float32) for shape in shapes),
        in_specs=[inside] * 3,
        out_specs=(inside, inside, scalar),
        name="finish",
    )(rotated, basis_slab, quotient)


def body(left_ops, right_ops, amplitudes, sketch, sector_shift):
    left_op = left_ops[0, 0]
    sectors = lax.axis_size("sec")
    height = amplitudes.shape[1]
    choice = lax.rem(sector_shift[0], sectors)
    flag = jnp.full((8, 128), choice.astype(jnp.float32))
    results = front(left_op, right_ops[0, 0], amplitudes[0], sketch, flag)
    rotated, basis_slab, energy = finish(*results)
    return (rotated[None, None], basis_slab[None], energy.reshape(()))


def solution(mesh):
    in_specs = (
        P("op", "sec", None, None),
        P("op", "sec", None, None),
        P("sec", "op", None),
        P(),
        P("op"),
    )
    out_specs = (P("op", "sec", None, None), P("sec", "op", None), P())
    return jax.shard_map(body, mesh=mesh, in_specs=in_specs, out_specs=out_specs, check_vma=False)
```
